256 devices in a mesh: row: 8 (over z), col: 32 (over y, x, core).
Axes of the slice: x: 4, y: 4, z: 8, core: 2. Of those that a mesh axis runs over, the one named last changes fastest.
Arguments:
- amps: bfloat16 [384, 131072], P('row', 'col'), may hold values from -6 to 6
- integrals: bfloat16 [131072, 8192], P('col', 'row'), may hold values from -0.046875 to 0.046875
- cd_first: int32 [131072], P('col'), may hold values from 0 to 2399
- cd_second: int32 [131072], P('col'), may hold values from 0 to 2399
- ab_first: int32 [8192], P('row'), may hold values from 0 to 2399
- ab_second: int32 [8192], P('row'), may hold values from 0 to 2399
- occ_first: int32 [384], P('col'), may hold values from 0 to 199
- occ_second: int32 [384], P('col'), may hold values from 0 to 199
- virt_irrep: int32 [2400], replicated, may hold values from 0 to 7
- occ_energy: float32 [200], replicated, may hold values from -2 to -0.5
- virt_energy: float32 [2400], replicated, may hold values from 0.2 to 3
Outputs:
- update: float32 [384, 8192], P('col', 'row')
The draws below stay inside these ranges and needn't reach their ends.
All inputs are finite; a program needn't handle non-finite values.
Results may differ from the reference program's by a relative error of at most 0.0003.
Values may be sent and summed in bfloat16 or wider, within the bound.
No kernel may reach another device: no remote copies, remote signals or barrier semaphores. Data moves between devices by JAX's collectives and lax.ppermute only.
A program may use at most 64 MiB of HBM per device.

```python
import jax
import jax.numpy as jnp
from jax import lax

NOCC = 200
NVIRT = 2400
PANEL = 128
OCC_PAIRS = 384
KP_DEV = 32
KCD = 131072
VPAIRS = 8192


def with_ends(array, stream_key, least, largest):
    longest = array.shape.index(max(array.shape))
    spots = []
    for shift in (0, 1):
        where = [jax.random.randint(jax.random.fold_in(stream_key, axis), (), 0, length) for axis, length in enumerate(array.shape)]
        where[longest] = (where[longest] + shift) % array.shape[longest]
        spots.append(tuple(where))
    return array.at[spots[0]].set(least).at[spots[1]].set(largest)


def strengthened(values, own_key, source, target, parts, factor):
    owner, partner = [(jnp.arange(values.shape[axis_at]) // (values.shape[axis_at] // parts)).reshape([-1 if axis == axis_at else 1 for axis in range(values.ndim)]) for axis_at in (source, target)]
    chosen = jax.random.permutation(own_key, parts)[partner]
    strong = (owner == chosen) | (owner == (partner + parts // 2) % parts)
    return jnp.where(strong, factor * values, values)


def block_scale(key, extent, shards, smallest, top_value):
    def one(dim, parts):
        draws = jax.random.uniform(jax.random.fold_in(jax.random.fold_in(key, 6), dim), (parts,), jnp.float32, smallest / len(shards), top_value / len(shards))
        return jnp.repeat(jnp.exp(draws), extent[dim] // parts).reshape((-1,) + (1,) * (len(extent) - dim - 1))

    gain = one(*shards[0])
    for cut in shards[1:]:
        gain = gain * one(*cut)
    return gain


def scatter_about(key, shape, deviation, reach, split=(), dtype=jnp.bfloat16):
    entries = deviation * jax.random.normal(key, shape, jnp.float32)
    if split:
        entries = entries * block_scale(key, shape, split, -0.22, 0.18)
    return jnp.clip(entries, -reach, reach).astype(dtype)


def noise_with(own_key, dims, deviation, limit, pieces, heavy, dtype=jnp.bfloat16):
    entries = deviation * jax.random.normal(own_key, dims, jnp.float32)
    if pieces:
        entries = entries * block_scale(own_key, dims, pieces, -0.22, 0.18)
    return jnp.clip(strengthened(entries, jax.random.fold_in(own_key, 3), *heavy), -limit, limit).astype(dtype)


def setup_inputs(seed: int = 0) -> dict:
    key_of = jax.random.split(jax.random.key(seed), 12)
    amps = noise_with(key_of[0], (OCC_PAIRS, KCD), 1.0, 6.0, ((0, 8), (1, 32)), (1, 0, 32, 2.75))
    integrals = scatter_about(key_of[1], (KCD, VPAIRS), (KCD // 8) ** -0.5, 0.046875, ((0, 32), (1, 8)))
    cd_first = with_ends(jax.random.randint(key_of[2], (KCD,), 0, NVIRT), jax.random.fold_in(key_of[2], 1), 0, NVIRT - 1).astype(jnp.int32)
    cd_second = with_ends(jax.random.randint(key_of[3], (KCD,), 0, NVIRT), jax.random.fold_in(key_of[3], 1), 0, NVIRT - 1).astype(jnp.int32)
    ab_first = with_ends(jax.random.randint(key_of[4], (VPAIRS,), 0, NVIRT), jax.random.fold_in(key_of[4], 1), 0, NVIRT - 1).astype(jnp.int32)
    ab_second = with_ends(jax.random.randint(key_of[5], (VPAIRS,), 0, NVIRT), jax.random.fold_in(key_of[5], 1), 0, NVIRT - 1).astype(jnp.int32)
    occ_first = with_ends(jax.random.randint(key_of[6], (OCC_PAIRS,), 0, NOCC), jax.random.fold_in(key_of[6], 1), 0, NOCC - 1).astype(jnp.int32)
    occ_second = with_ends(jax.random.randint(key_of[7], (OCC_PAIRS,), 0, NOCC), jax.random.fold_in(key_of[7], 1), 0, NOCC - 1).astype(jnp.int32)
    virt_irrep = with_ends(jax.random.randint(key_of[8], (NVIRT,), 0, 8), jax.random.fold_in(key_of[8], 1), 0, 7).astype(jnp.int32)
    occ_energy = jnp.clip(jax.random.uniform(key_of[9], (NOCC,), jnp.float32, -2.0, -0.5), -2.0, -0.5)
    virt_energy = jnp.clip(jax.random.uniform(key_of[10], (NVIRT,), jnp.float32, 0.2, 3.0), 0.2, 3.0)
    return dict(amps=amps, integrals=integrals, cd_first=cd_first, cd_second=cd_second, ab_first=ab_first, ab_second=ab_second, occ_first=occ_first, occ_second=occ_second, virt_irrep=virt_irrep, occ_energy=occ_energy, virt_energy=virt_energy)


def reference(amps, integrals, cd_first, cd_second, ab_first, ab_second, occ_first, occ_second, virt_irrep, occ_energy, virt_energy):
    irrep_cd = jnp.bitwise_xor(jnp.take(virt_irrep, cd_first), jnp.take(virt_irrep, cd_second))
    irrep_ab = jnp.bitwise_xor(jnp.take(virt_irrep, ab_first), jnp.take(virt_irrep, ab_second))
    block = PANEL * KP_DEV
    count = KCD // block

    def add_block(index, total):
        start = (index * block).astype(jnp.int32)
        left = lax.dynamic_slice_in_dim(amps, start, block, 1)
        right = lax.dynamic_slice_in_dim(integrals, start, block, 0)
        labels = lax.dynamic_slice_in_dim(irrep_cd, start, block, 0)
        masked = jnp.where(labels[:, None] == irrep_ab[None, :], right, jnp.zeros_like(right))
        return total + jnp.dot(left, masked, preferred_element_type=jnp.float32)

    ladder = lax.fori_loop(0, count, add_block, jnp.zeros((OCC_PAIRS, VPAIRS), jnp.float32))
    virt_part = jnp.take(virt_energy, ab_first) + jnp.take(virt_energy, ab_second)
    occ_part = jnp.take(occ_energy, occ_first) + jnp.take(occ_energy, occ_second)
    denom = virt_part[None, :] - occ_part[:, None]
    return ladder / denom
```

```python
import jax
import jax.numpy as jnp
from jax import lax
from jax.experimental import pallas as pl
from jax.experimental.pallas import tpu as pltpu
from jax.sharding import Mesh, PartitionSpec as P

LANES = 128
K_BLOCK = 512
ORDER = (0, -1, 1, -2, 2, -3, 3, 4)


def lookup(table_ref, rows, index):
    high = index // LANES
    low = index % LANES
    picked = jnp.zeros(index.shape, table_ref.dtype)
    for row in range(rows):
        line = jnp.broadcast_to(table_ref[row : row + 1, :], index.shape)
        value = jnp.take_along_axis(line, low, axis=1, mode="promise_in_bounds")
        picked = jnp.where(high == row, value, picked)
    return picked


def tables_kernel(cd1, cd2, ab1, ab2, occ, irrep, virt, occ_energy, cd_out, ab_out, virt_out, occ_out):
    rows = irrep.shape[0]
    for tile in range(cd1.shape[0] // 8):
        part = slice(8 * tile, 8 * tile + 8)
        label = lookup(irrep, rows, cd1[part, :]) ^ lookup(irrep, rows, cd2[part, :])
        cd_out[part, :] = label.astype(jnp.float32)
    label = lookup(irrep, rows, ab1[...]) ^ lookup(irrep, rows, ab2[...])
    ab_out[...] = label.astype(jnp.float32)
    virt_out[...] = lookup(virt, rows, ab1[...]) + lookup(virt, rows, ab2[...])
    picked = lookup(occ_energy, occ_energy.shape[0], occ[...])
    both = picked[0:1, :] + picked[1:2, :]
    column = jnp.broadcast_to(both, (LANES, LANES)).T
    occ_out[...] = column[: occ_out.shape[0], :]


def ladder_kernel(where, cd, ab, values, own, *refs):
    pieces = refs[:14]
    keep, send, total, masked = refs[14:]
    step = pl.program_id(0)
    steps = pl.num_programs(0)

    @pl.when(step == 0)
    def _():
        total[...] = jnp.zeros_like(total)

    for part in range(K_BLOCK // LANES):
        line = cd[pl.ds(step * (K_BLOCK // LANES) + part, 1), :]
        label = jnp.broadcast_to(line, (LANES, LANES)).T.astype(jnp.bfloat16)
        down = slice(part * LANES, part * LANES + LANES)
        for lane in range(values.shape[1] // LANES):
            across = slice(lane * LANES, lane * LANES + LANES)
            other = jnp.broadcast_to(ab[lane : lane + 1, :], (LANES, LANES)).astype(jnp.bfloat16)
            block = values[down, across]
            masked[down, across] = jnp.where(label == other, block, jnp.zeros_like(block))

    def accumulate(half):
        offset = pl.multiple_of((step - half * (steps // 2)) * K_BLOCK, K_BLOCK)
        left = [own[:, pl.ds(pl.multiple_of(step * K_BLOCK, K_BLOCK), K_BLOCK)]]
        left += [pieces[2 * i + half][:, pl.ds(offset, K_BLOCK)] for i in range(7)]
        total[...] += jnp.dot(
            jnp.concatenate(left, axis=0), masked[...], preferred_element_type=jnp.float32
        )

    @pl.when(step < steps // 2)
    def _():
        accumulate(0)

    @pl.when(step >= steps // 2)
    def _():
        accumulate(1)

    @pl.when(step == steps - 1)
    def _():
        layer = where[0]
        first_core = where[1] == 0
        rows = own.shape[0] // 4
        for place, shift in enumerate(ORDER):
            shard = lax.rem(layer + (shift + 8), 8)
            for high in range(2):
                at = place * own.shape[0] + 2 * high * rows
                even = total[at : at + rows, :]
                odd = total[at + rows : at + 2 * rows, :]
                kept = jnp.where(first_core, even, odd)
                sent = jnp.where(first_core, odd, even)
                for lane in range(kept.shape[1] // LANES):
                    across = slice(lane * LANES, lane * LANES + LANES)
                    down = slice(lane * rows, lane * rows + rows)
                    keep[2 * shard + high, down, :] = kept[:, across]
                    send[2 * shard + high, down, :] = sent[:, across]


def finish_kernel(parts, virt, occ, out):
    rows = out.shape[0]
    summed = jnp.sum(parts[...], axis=0)
    for lane in range(out.shape[1] // LANES):
        ladder = summed[lane * rows : lane * rows + rows, :]
        denom = virt[lane : lane + 1, :] - occ[:rows, :]
        out[:, lane * LANES : lane * LANES + LANES] = ladder / denom


def as_table(values):
    size = -(-values.shape[0] // 1024) * 1024
    return jnp.pad(values, (0, size - values.shape[0])).reshape(size // LANES, LANES)


def on_device(amps, integrals, cd1, cd2, ab1, ab2, occ1, occ2, irrep, occ_energy, virt_energy):
    depth = amps.shape[1]
    width = integrals.shape[1]
    rows = occ1.shape[0]
    forward = [(i, (i + 1) % 8) for i in range(8)]
    backward = [(i, (i - 1) % 8) for i in range(8)]
    up = [amps[:, : depth // 2], amps[:, depth // 2 :]]
    down = list(up)
    pieces = []
    for _ in range(3):
        up[0] = lax.ppermute(up[0], "z", forward)
        up[1] = lax.ppermute(up[1], "z", forward)
        down[0] = lax.ppermute(down[0], "z", backward)
        down[1] = lax.ppermute(down[1], "z", backward)
        pieces += up + down
    pieces += [lax.ppermute(up[0], "z", forward), lax.ppermute(down[1], "z", backward)]

    vmem = pl.BlockSpec(memory_space=pltpu.VMEM)
    occ = jnp.zeros((8, LANES), jnp.int32)
    occ = occ.at[0, :rows].set(occ1).at[1, :rows].set(occ2)
    square = lambda x: x.reshape(x.shape[0] // LANES, LANES)
    cd, ab, virt, occ_part = pl.pallas_call(
        tables_kernel,
        out_shape=(
            jax.ShapeDtypeStruct((depth // LANES, LANES), jnp.float32),
            jax.ShapeDtypeStruct((width // LANES, LANES), jnp.float32),
            jax.ShapeDtypeStruct((width // LANES, LANES), jnp.float32),
            jax.ShapeDtypeStruct((16, LANES), jnp.float32),
        ),
        in_specs=[vmem] * 8,
        out_specs=(vmem,) * 4,
    )(
        square(cd1), square(cd2), square(ab1), square(ab2), occ,
        as_table(irrep), as_table(virt_energy), as_table(occ_energy),
    )

    where = jnp.stack([lax.axis_index("z"), lax.axis_index("core")]).astype(jnp.int32)
    block = jax.ShapeDtypeStruct((16, rows * width // LANES, LANES), jnp.float32)
    keep, send = pl.pallas_call(
        ladder_kernel,
        out_shape=(block, block),
        grid_spec=pltpu.PrefetchScalarGridSpec(
            num_scalar_prefetch=1,
            grid=(depth // K_BLOCK,),
            in_specs=[vmem, vmem, pl.BlockSpec((K_BLOCK, width), lambda k, where: (k, 0)), vmem]
            + [vmem] * 14,
            out_specs=(vmem, vmem),
            scratch_shapes=[
                pltpu.VMEM((8 * amps.shape[0], width), jnp.float32),
                pltpu.VMEM((K_BLOCK, width), jnp.bfloat16),
            ],
        ),
        compiler_params=pltpu.CompilerParams(vmem_limit_bytes=32 * 1024 * 1024),
    )(where, cd, ab, integrals, amps, *pieces)

    both = keep + lax.ppermute(send, "core", [(0, 1), (1, 0)])
    parts = lax.all_to_all(both, ("y", "x"), 0, 0, tiled=True)
    return pl.pallas_call(
        finish_kernel,
        out_shape=jax.ShapeDtypeStruct((rows, width), jnp.float32),
        in_specs=[vmem] * 3,
        out_specs=vmem,
    )(parts, virt, occ_part)


def solution(mesh):
    fine = Mesh(mesh.devices.reshape(8, 4, 4, 2), ("z", "y", "x", "core"))
    col = ("y", "x", "core")
    in_specs = (
        P("z", col), P(col, "z"), P(col), P(col), P("z"), P("z"), P(col), P(col), P(), P(), P(),
    )
    return jax.shard_map(
        on_device, mesh=fine, in_specs=in_specs, out_specs=P(col, "z"), check_vma=False
    )
```

```python
import jax
import jax.numpy as jnp
from jax import lax
from jax.experimental import pallas as pl
from jax.experimental.pallas import tpu as pltpu
from jax.sharding import Mesh, PartitionSpec as P

LANES = 128
K_BLOCK = 1024
FIRST = (0, -1, -1, 1, 1, -2, -2, 2, 2, -3, -3, 3, 3)
SHARDS = (0, -1, 1, -2, 2, -3, 3)
MIB = 1024 * 1024


def lookup(table_ref, index):
    size = table_ref.shape[0]
    high = index // LANES
    low = index % LANES
    picked = jnp.zeros(index.shape, table_ref.dtype)
    for row in range(-(-size // LANES)):
        line = table_ref[pl.ds(row * LANES, min(LANES, size - row * LANES))].reshape(1, -1)
        if line.shape[1] < LANES:
            line = jnp.pad(line, ((0, 0), (0, LANES - line.shape[1])))
        line = jnp.broadcast_to(line, index.shape)
        value = jnp.take_along_axis(line, low, axis=1, mode="promise_in_bounds")
        picked = jnp.where(high == row, value, picked)
    return picked


def tables_kernel(cd1, cd2, ab1, ab2, occ1, occ2, irrep, virt, energy, cd_out, ab_out, virt_out, occ_out):
    for tile in range(cd1.shape[0] // 8):
        part = slice(8 * tile, 8 * tile + 8)
        label = lookup(irrep, cd1[part, :]) ^ lookup(irrep, cd2[part, :])
        cd_out[part, :] = label.astype(jnp.float32)
    label = lookup(irrep, ab1[...]) ^ lookup(irrep, ab2[...])
    ab_out[...] = label.astype(jnp.float32)
    virt_out[...] = lookup(virt, ab1[...]) + lookup(virt, ab2[...])
    for row in range(occ1.shape[0]):
        both = energy[occ1[row]] + energy[occ2[row]]
        occ_out[row : row + 1, :] = jnp.full((1, LANES), both, jnp.float32)


def spread(where, total, place, shard, rows, keep, send):
    first_core = where[1] == 0
    for high in range(2):
        at = place * 4 * rows + 2 * high * rows
        even = total[at : at + rows, :]
        odd = total[at + rows : at + 2 * rows, :]
        kept = jnp.where(first_core, even, odd)
        sent = jnp.where(first_core, odd, even)
        for lane in range(kept.shape[1] // LANES):
            across = slice(lane * LANES, lane * LANES + LANES)
            down = slice(lane * rows, lane * rows + rows)
            keep[2 * shard + high, down, :] = kept[:, across]
            send[2 * shard + high, down, :] = sent[:, across]


def first_kernel(where, cd, ab, values, *refs):
    pieces = refs[:14]
    keep, send, masked, total = refs[14:]
    step = pl.program_id(0)
    steps = pl.num_programs(0)

    @pl.when(step == 0)
    def _():
        total[...] = jnp.zeros_like(total)

    base = pl.multiple_of(step * K_BLOCK, K_BLOCK)
    other = ab[...].astype(jnp.bfloat16)
    for part in range(K_BLOCK // LANES):
        line = cd[pl.ds(step * (K_BLOCK // LANES) + part, 1), :]
        label = jnp.broadcast_to(line, (LANES, LANES)).T.astype(jnp.bfloat16)
        down = slice(part * LANES, part * LANES + LANES)
        for lane in range(values.shape[1] // LANES):
            across = slice(lane * LANES, lane * LANES + LANES)
            block = values[down, across]
            same = label == jnp.broadcast_to(other[lane : lane + 1, :], (LANES, LANES))
            masked[pl.ds(base + part * LANES, LANES), across] = jnp.where(
                same, block, jnp.zeros_like(block)
            )

    def accumulate(half):
        offset = pl.multiple_of((step - half * (steps // 2)) * K_BLOCK, K_BLOCK)
        left = [pieces[2 * i + half][:, pl.ds(offset, K_BLOCK)] for i in range(7)]
        total[...] += jnp.dot(
            jnp.concatenate(left, axis=0),
            masked[pl.ds(base, K_BLOCK), :],
            preferred_element_type=jnp.float32,
        )

    @pl.when(step < steps // 2)
    def _():
        accumulate(0)

    @pl.when(step >= steps // 2)
    def _():
        accumulate(1)

    @pl.when(step == steps - 1)
    def _():
        for place, shift in enumerate(SHARDS):
            shard = lax.rem(where[0] + (shift + 8), 8)
            spread(where, total, place, shard, pieces[0].shape[0] // 4, keep, send)


def last_kernel(where, masked, left, right, keep_in, send_in, keep, send, total):
    half = left.shape[1]
    total[...] = jnp.dot(left[...], masked[:half, :], preferred_element_type=jnp.float32)
    total[...] += jnp.dot(right[...], masked[half:, :], preferred_element_type=jnp.float32)
    keep[...] = keep_in[...]
    send[...] = send_in[...]
    spread(where, total, 0, lax.rem(where[0] + 4, 8), left.shape[0] // 4, keep, send)


def pack_kernel(keep, got, out):
    rows = keep.shape[1]
    for block in range(keep.shape[0]):
        both = keep[block] + got[block]
        top = jnp.maximum(jnp.max(jnp.abs(both), axis=0, keepdims=True), 1e-30)
        power = jnp.floor(14.99 - jnp.log2(top))
        scaled = jnp.clip(jnp.round(both * jnp.exp2(power)), -32767.0, 32767.0)
        out[block, :rows, :] = scaled.astype(jnp.int32).astype(jnp.int16)
        power = jnp.broadcast_to(power, (out.shape[1] - rows, LANES))
        out[block, rows:, :] = power.astype(jnp.int32).astype(jnp.int16)


def finish_kernel(parts, virt, occ, out):
    rows = out.shape[0]
    size = rows * out.shape[1] // LANES
    summed = jnp.zeros((size, LANES), jnp.float32)
    for block in range(parts.shape[0]):
        power = parts[block, size:, :].astype(jnp.int32).astype(jnp.float32)
        value = parts[block, :size, :].astype(jnp.int32).astype(jnp.float32)
        summed += value * jnp.exp2(-power[0:1, :])
    for lane in range(out.shape[1] // LANES):
        ladder = summed[lane * rows : lane * rows + rows, :]
        denom = virt[lane : lane + 1, :] - occ[:rows, :]
        out[:, lane * LANES : lane * LANES + LANES] = ladder / denom


def on_device(amps, integrals, cd1, cd2, ab1, ab2, occ1, occ2, irrep, occ_energy, virt_energy):
    depth = amps.shape[1]
    width = integrals.shape[1]
    rows = occ1.shape[0]
    forward = [(i, (i + 1) % 8) for i in range(8)]
    backward = [(i, (i - 1) % 8) for i in range(8)]
    up = [amps[:, : depth // 2], amps[:, depth // 2 :]]
    down = list(up)
    pieces = list(up)
    for _ in range(3):
        up[0] = lax.ppermute(up[0], "z", forward)
        up[1] = lax.ppermute(up[1], "z", forward)
        down[0] = lax.ppermute(down[0], "z", backward)
        down[1] = lax.ppermute(down[1], "z", backward)
        pieces += up + down
    last = [lax.ppermute(up[0], "z", forward), lax.ppermute(down[1], "z", backward)]

    vmem = pl.BlockSpec(memory_space=pltpu.VMEM)
    smem = pl.BlockSpec(memory_space=pltpu.SMEM)
    square = lambda x: x.reshape(x.shape[0] // LANES, LANES)
    cd, ab, virt, occ = pl.pallas_call(
        tables_kernel,
        out_shape=(
            pltpu.VMEM((depth // LANES, LANES), jnp.float32),
            pltpu.VMEM((width // LANES, LANES), jnp.float32),
            pltpu.VMEM((width // LANES, LANES), jnp.float32),
            pltpu.VMEM((16, LANES), jnp.float32),
        ),
        in_specs=[vmem] * 4 + [smem] * 2 + [vmem] * 2 + [smem],
        out_specs=(vmem,) * 4,
        compiler_params=pltpu.CompilerParams(vmem_limit_bytes=4 * MIB),
    )(
        *[pltpu.with_memory_space_constraint(x, pltpu.HBM) for x in (
            square(cd1), square(cd2), square(ab1), square(ab2), occ1, occ2,
            irrep, virt_energy, occ_energy,
        )]
    )

    where = jnp.stack([lax.axis_index("z"), lax.axis_index("core")]).astype(jnp.int32)
    block = pltpu.VMEM((16, rows * width // LANES, LANES), jnp.float32)
    keep, send, masked = pl.pallas_call(
        first_kernel,
        out_shape=(block, block, pltpu.VMEM((depth, width), jnp.bfloat16)),
        grid_spec=pltpu.PrefetchScalarGridSpec(
            num_scalar_prefetch=1,
            grid=(depth // K_BLOCK,),
            in_specs=[vmem, vmem, pl.BlockSpec((K_BLOCK, width), lambda k, where: (k, 0))]
            + [vmem] * 14,
            out_specs=(vmem, vmem, vmem),
            scratch_shapes=[pltpu.VMEM((7 * amps.shape[0], width), jnp.float32)],
        ),
        compiler_params=pltpu.CompilerParams(vmem_limit_bytes=20 * MIB),
    )(where, cd, ab, pltpu.with_memory_space_constraint(integrals, pltpu.HBM), *pieces)
    keep, send = pl.pallas_call(
        last_kernel,
        out_shape=(block, block),
        grid_spec=pltpu.PrefetchScalarGridSpec(
            num_scalar_prefetch=1,
            grid=(),
            in_specs=[vmem] * 5,
            out_specs=(vmem, vmem),
            scratch_shapes=[pltpu.VMEM((amps.shape[0], width), jnp.float32)],
        ),
        input_output_aliases={4: 0, 5: 1},
        compiler_params=pltpu.CompilerParams(vmem_limit_bytes=20 * MIB),
    )(where, masked, *last, keep, send)

    got = lax.ppermute(send, "core", [(0, 1), (1, 0)])
    packed = pl.pallas_call(
        pack_kernel,
        out_shape=pltpu.VMEM((16, block.shape[1] + 16, LANES), jnp.int16),
        in_specs=[vmem] * 2,
        out_specs=vmem,
        compiler_params=pltpu.CompilerParams(vmem_limit_bytes=4 * MIB),
    )(keep, got)
    parts = lax.all_to_all(packed, ("y", "x"), 0, 0, tiled=True)
    return pl.pallas_call(
        finish_kernel,
        out_shape=jax.ShapeDtypeStruct((rows, width), jnp.float32),
        in_specs=[vmem] * 3,
        out_specs=vmem,
        compiler_params=pltpu.CompilerParams(vmem_limit_bytes=4 * MIB),
    )(parts, virt, occ)


def solution(mesh):
    fine = Mesh(mesh.devices.reshape(8, 4, 4, 2), ("z", "y", "x", "core"))
    col = ("y", "x", "core")
    in_specs = (
        P("z", col), P(col, "z"), P(col), P(col), P("z"), P("z"), P(col), P(col), P(), P(), P(),
    )
    return jax.shard_map(
        on_device, mesh=fine, in_specs=in_specs, out_specs=P(col, "z"), check_vma=False
    )
```

```python
import jax
import jax.numpy as jnp
from jax import lax
from jax.experimental import pallas as pl
from jax.experimental.pallas import tpu as pltpu
from jax.sharding import Mesh, PartitionSpec as P

LANES = 128
K_BLOCK = 1024
MIB = 1024 * 1024


def lookup(table_ref, index):
    size = table_ref.shape[0]
    high = index // LANES
    low = index % LANES
    picked = jnp.zeros(index.shape, table_ref.dtype)
    for row in range(-(-size // LANES)):
        line = table_ref[pl.ds(row * LANES, min(LANES, size - row * LANES))].reshape(1, -1)
        if line.shape[1] < LANES:
            line = jnp.pad(line, ((0, 0), (0, LANES - line.shape[1])))
        line = jnp.broadcast_to(line, index.shape)
        value = jnp.take_along_axis(line, low, axis=1, mode="promise_in_bounds")
        picked = jnp.where(high == row, value, picked)
    return picked


def tables_kernel(cd1, cd2, ab1, ab2, occ1, occ2, irrep, virt, energy, cd_out, ab_out, virt_out, occ_out):
    for tile in range(cd1.shape[0] // 8):
        part = slice(8 * tile, 8 * tile + 8)
        label = lookup(irrep, cd1[part, :]) ^ lookup(irrep, cd2[part, :])
        cd_out[part, :] = label.astype(jnp.float32)
    label = lookup(irrep, ab1[...]) ^ lookup(irrep, ab2[...])
    ab_out[...] = label.astype(jnp.float32)
    virt_out[...] = lookup(virt, ab1[...]) + lookup(virt, ab2[...])
    for row in range(occ1.shape[0]):
        both = energy[occ1[row]] + energy[occ2[row]]
        occ_out[row : row + 1, :] = jnp.full((1, LANES), both, jnp.float32)


def spread(where, total, place, offset, rows, keep, send):
    first_core = where[2] == 0
    shard = lax.rem(where[0] + where[1] * offset + 8, 8)
    for high in range(2):
        at = place * 4 * rows + 2 * high * rows
        even = total[at : at + rows, :]
        odd = total[at + rows : at + 2 * rows, :]
        kept = jnp.where(first_core, even, odd)
        sent = jnp.where(first_core, odd, even)
        for lane in range(kept.shape[1] // LANES):
            across = slice(lane * LANES, lane * LANES + LANES)
            down = slice(lane * rows, lane * rows + rows)
            keep[2 * shard + high, down, :] = kept[:, across]
            send[2 * shard + high, down, :] = sent[:, across]


def mask_kernel(cd, ab, values, masked, ready):
    step = pl.program_id(0)
    ready[...] = jnp.zeros_like(ready)
    base = pl.multiple_of(step * K_BLOCK, K_BLOCK)
    other = ab[...].astype(jnp.bfloat16)
    for part in range(K_BLOCK // LANES):
        line = cd[pl.ds(step * (K_BLOCK // LANES) + part, 1), :]
        label = jnp.broadcast_to(line, (LANES, LANES)).T.astype(jnp.bfloat16)
        down = slice(part * LANES, part * LANES + LANES)
        for lane in range(values.shape[1] // LANES):
            across = slice(lane * LANES, lane * LANES + LANES)
            block = values[down, across]
            same = label == jnp.broadcast_to(other[lane : lane + 1, :], (LANES, LANES))
            masked[pl.ds(base + part * LANES, LANES), across] = jnp.where(
                same, block, jnp.zeros_like(block)
            )


def dot_into(total, masked, left, right):
    half = masked.shape[0] // 2
    total[...] = jnp.dot(
        jnp.concatenate(left, axis=0), masked[:half, :], preferred_element_type=jnp.float32
    )
    total[...] += jnp.dot(
        jnp.concatenate(right, axis=0), masked[half:, :], preferred_element_type=jnp.float32
    )


def first_kernel(where, ready, masked, a1, b1, a2, b2, a3, b3, keep, send, total):
    size = a2.shape[0] // 2
    left = [a1[...], a2[...], a3[:size, :]]
    right = [b1[:size, :], b2[:size, :], b1[size:, :], b3[:size, :], b2[size:, :]]
    dot_into(total, masked, left, right)
    for place, offset in enumerate((0, 1, -1, -2, 2)):
        spread(where, total, place, offset, size // 4, keep, send)


def last_kernel(where, masked, a3, b3, a4, b4, keep_in, send_in, keep, send, total):
    size = a4.shape[0] // 2
    left = [a3[size:, :], a4[...]]
    right = [b4[:size, :], b3[size:, :], b4[size:, :]]
    dot_into(total, masked, left, right)
    keep[...] = keep_in[...]
    send[...] = send_in[...]
    for place, offset in enumerate((3, -3, 4)):
        spread(where, total, place, offset, size // 4, keep, send)


def pack_kernel(keep, got, out):
    rows = keep.shape[1]
    for block in range(keep.shape[0]):
        both = keep[block] + got[block]
        top = jnp.maximum(jnp.max(jnp.abs(both), axis=0, keepdims=True), 1e-30)
        power = jnp.floor(14.99 - jnp.log2(top))
        scaled = jnp.clip(jnp.round(both * jnp.exp2(power)), -32767.0, 32767.0)
        out[block, :rows, :] = scaled.astype(jnp.int32).astype(jnp.int16)
        power = jnp.broadcast_to(power, (out.shape[1] - rows, LANES))
        out[block, rows:, :] = power.astype(jnp.int32).astype(jnp.int16)


def finish_kernel(parts, virt, occ, out):
    rows = out.shape[0]
    size = rows * out.shape[1] // LANES
    summed = jnp.zeros((size, LANES), jnp.float32)
    for block in range(parts.shape[0]):
        power = parts[block, size:, :].astype(jnp.int32).astype(jnp.float32)
        value = parts[block, :size, :].astype(jnp.int32).astype(jnp.float32)
        summed += value * jnp.exp2(-power[0:1, :])
    for lane in range(out.shape[1] // LANES):
        ladder = summed[lane * rows : lane * rows + rows, :]
        denom = virt[lane : lane + 1, :] - occ[:rows, :]
        out[:, lane * LANES : lane * LANES + LANES] = ladder / denom


def on_device(amps, integrals, cd1, cd2, ab1, ab2, occ1, occ2, irrep, occ_energy, virt_energy):
    depth = amps.shape[1]
    width = integrals.shape[1]
    rows = occ1.shape[0]
    vmem = pl.BlockSpec(memory_space=pltpu.VMEM)
    smem = pl.BlockSpec(memory_space=pltpu.SMEM)
    square = lambda x: x.reshape(x.shape[0] // LANES, LANES)
    cd, ab, virt, occ = pl.pallas_call(
        tables_kernel,
        out_shape=(
            pltpu.VMEM((depth // LANES, LANES), jnp.float32),
            pltpu.VMEM((width // LANES, LANES), jnp.float32),
            pltpu.VMEM((width // LANES, LANES), jnp.float32),
            pltpu.VMEM((16, LANES), jnp.float32),
        ),
        in_specs=[vmem] * 4 + [smem] * 2 + [vmem] * 2 + [smem],
        out_specs=(vmem,) * 4,
        compiler_params=pltpu.CompilerParams(vmem_limit_bytes=4 * MIB),
    )(
        *[pltpu.with_memory_space_constraint(x, pltpu.HBM) for x in (
            square(cd1), square(cd2), square(ab1), square(ab2), occ1, occ2,
            irrep, virt_energy, occ_energy,
        )]
    )

    layer = lax.axis_index("z")
    where = jnp.stack([layer, 1 - 2 * (layer % 2), lax.axis_index("core")]).astype(jnp.int32)
    masked, ready = pl.pallas_call(
        mask_kernel,
        out_shape=(pltpu.VMEM((depth, width), jnp.bfloat16), pltpu.VMEM((8, LANES), jnp.float32)),
        grid=(depth // K_BLOCK,),
        in_specs=[vmem, vmem, pl.BlockSpec((K_BLOCK, width), lambda k: (k, 0))],
        out_specs=(vmem, vmem),
        compiler_params=pltpu.CompilerParams(vmem_limit_bytes=8 * MIB),
    )(cd, ab, pltpu.with_memory_space_constraint(integrals, pltpu.HBM))
    inner = [(i, i ^ 1) for i in range(8)]
    outer = [(i, (i - 1 if i % 2 == 0 else i + 1) % 8) for i in range(8)]
    a0, b0 = amps[:, : depth // 2], amps[:, depth // 2 :]
    a1 = jnp.concatenate([a0, lax.ppermute(a0, "z", inner)], axis=0)
    b1 = jnp.concatenate([b0, lax.ppermute(b0, "z", outer)], axis=0)
    b1, where = lax.optimization_barrier((b1, where))
    a2, b2 = lax.ppermute(a1, "z", outer), lax.ppermute(b1, "z", inner)
    a2, ready = lax.optimization_barrier((a2, ready))
    a3, b3 = lax.ppermute(a2, "z", inner), lax.ppermute(b2, "z", outer)
    a4, b4 = lax.ppermute(a3, "z", outer), lax.ppermute(b3, "z", inner)

    block = pltpu.VMEM((16, rows * width // LANES, LANES), jnp.float32)
    keep, send = pl.pallas_call(
        first_kernel,
        out_shape=(block, block),
        grid_spec=pltpu.PrefetchScalarGridSpec(
            num_scalar_prefetch=1,
            grid=(),
            in_specs=[vmem] * 8,
            out_specs=(vmem, vmem),
            scratch_shapes=[pltpu.VMEM((5 * amps.shape[0], width), jnp.float32)],
        ),
        compiler_params=pltpu.CompilerParams(vmem_limit_bytes=16 * MIB),
    )(where, ready, masked, a1, b1, a2, b2, a3, b3)
    keep, send = pl.pallas_call(
        last_kernel,
        out_shape=(block, block),
        grid_spec=pltpu.PrefetchScalarGridSpec(
            num_scalar_prefetch=1,
            grid=(),
            in_specs=[vmem] * 7,
            out_specs=(vmem, vmem),
            scratch_shapes=[pltpu.VMEM((3 * amps.shape[0], width), jnp.float32)],
        ),
        input_output_aliases={6: 0, 7: 1},
        compiler_params=pltpu.CompilerParams(vmem_limit_bytes=16 * MIB),
    )(where, masked, a3, b3, a4, b4, keep, send)

    got = lax.ppermute(send, "core", [(0, 1), (1, 0)])
    packed = pl.pallas_call(
        pack_kernel,
        out_shape=pltpu.VMEM((16, block.shape[1] + 16, LANES), jnp.int16),
        in_specs=[vmem] * 2,
        out_specs=vmem,
        compiler_params=pltpu.CompilerParams(vmem_limit_bytes=4 * MIB),
    )(keep, got)
    parts = lax.all_to_all(packed, ("y", "x"), 0, 0, tiled=True)
    return pl.pallas_call(
        finish_kernel,
        out_shape=jax.ShapeDtypeStruct((rows, width), jnp.float32),
        in_specs=[vmem] * 3,
        out_specs=vmem,
        compiler_params=pltpu.CompilerParams(vmem_limit_bytes=4 * MIB),
    )(parts, virt, occ)


def solution(mesh):
    fine = Mesh(mesh.devices.reshape(8, 4, 4, 2), ("z", "y", "x", "core"))
    col = ("y", "x", "core")
    in_specs = (
        P("z", col), P(col, "z"), P(col), P(col), P("z"), P("z"), P(col), P(col), P(), P(), P(),
    )
    return jax.shard_map(
        on_device, mesh=fine, in_specs=in_specs, out_specs=P(col, "z"), check_vma=False
    )
```

```python
import jax
import jax.numpy as jnp
from jax import lax
from jax.experimental import pallas as pl
from jax.experimental.pallas import tpu as pltpu
from jax.sharding import Mesh, PartitionSpec as P

LANES = 128
MIB = 1024 * 1024


def lookup(table_ref, index):
    size = table_ref.shape[0]
    high = index // LANES
    low = index % LANES
    picked = jnp.zeros(index.shape, table_ref.dtype)
    for row in range(-(-size // LANES)):
        line = table_ref[pl.ds(row * LANES, min(LANES, size - row * LANES))].reshape(1, -1)
        if line.shape[1] < LANES:
            line = jnp.pad(line, ((0, 0), (0, LANES - line.shape[1])))
        line = jnp.broadcast_to(line, index.shape)
        value = jnp.take_along_axis(line, low, axis=1, mode="promise_in_bounds")
        picked = jnp.where(high == row, value, picked)
    return picked


def mask_kernel(cd1, cd2, ab1, ab2, occ1, occ2, irrep, virt, energy, values, masked, virt_out, occ_out, arrived):
    blocks = arrived.shape[0]
    size = values.shape[0] // blocks
    copies = []
    for block in range(blocks):
        down = pl.ds(block * size, size)
        copies.append(
            pltpu.make_async_copy(values.at[down, :], masked.at[down, :], arrived.at[block])
        )
        copies[-1].start()

    virt_out[...] = lookup(virt, ab1[...]) + lookup(virt, ab2[...])
    for row in range(occ1.shape[0]):
        both = energy[occ1[row]] + energy[occ2[row]]
        occ_out[row : row + 1, :] = jnp.full((1, LANES), both, jnp.float32)
    label = lookup(irrep, ab1[...]) ^ lookup(irrep, ab2[...])
    other = label.astype(jnp.float32).astype(jnp.bfloat16)
    other = [jnp.broadcast_to(other[i : i + 1, :], (LANES, LANES)) for i in range(ab1.shape[0])]
    labels = []
    for tile in range(cd1.shape[0] // 8):
        part = slice(8 * tile, 8 * tile + 8)
        label = lookup(irrep, cd1[part, :]) ^ lookup(irrep, cd2[part, :])
        labels.append(label.astype(jnp.float32))

    for block in range(blocks):
        copies[block].wait()
        for part in range(block * size // LANES, (block + 1) * size // LANES):
            line = labels[part // 8][part % 8 : part % 8 + 1, :]
            label = jnp.broadcast_to(line, (LANES, LANES)).T.astype(jnp.bfloat16)
            down = slice(part * LANES, part * LANES + LANES)
            for lane in range(masked.shape[1] // LANES):
                across = slice(lane * LANES, lane * LANES + LANES)
                piece = masked[down, across]
                masked[down, across] = jnp.where(
                    label == other[lane], piece, jnp.zeros_like(piece)
                )


def spread(where, total, place, offset, rows, keep, send):
    first_core = where[2] == 0
    shard = lax.rem(where[0] + where[1] * offset + 8, 8)
    for high in range(2):
        at = place * 4 * rows + 2 * high * rows
        even = total[at : at + rows, :]
        odd = total[at + rows : at + 2 * rows, :]
        kept = jnp.where(first_core, even, odd)
        sent = jnp.where(first_core, odd, even)
        for lane in range(kept.shape[1] // LANES):
            across = slice(lane * LANES, lane * LANES + LANES)
            down = slice(lane * rows, lane * rows + rows)
            keep[2 * shard + high, down, :] = kept[:, across]
            send[2 * shard + high, down, :] = sent[:, across]


def dot_into(total, masked, left, right):
    half = masked.shape[0] // 2
    total[...] = jnp.dot(
        jnp.concatenate(left, axis=0), masked[:half, :], preferred_element_type=jnp.float32
    )
    total[...] += jnp.dot(
        jnp.concatenate(right, axis=0), masked[half:, :], preferred_element_type=jnp.float32
    )


def first_kernel(where, ready, masked, a1, b1, a2, b2, a3, b3, keep, send, total):
    dot_into(total, masked, [a1[...], a2[...], a3[...]], [b1[...], b2[...], b3[...]])
    for place, offset in enumerate((0, 1, -1, -2, 2, 3)):
        spread(where, total, place, offset, a1.shape[0] // 8, keep, send)


def last_kernel(where, masked, a4, b4, keep_in, send_in, keep, send, total):
    dot_into(total, masked, [a4[...]], [b4[...]])
    keep[...] = keep_in[...]
    send[...] = send_in[...]
    for place, offset in enumerate((-3, -4)):
        spread(where, total, place, offset, a4.shape[0] // 8, keep, send)


def pack_kernel(keep, got, out):
    rows = keep.shape[1]
    for block in range(keep.shape[0]):
        both = keep[block] + got[block]
        top = jnp.maximum(jnp.max(jnp.abs(both), axis=0, keepdims=True), 1e-30)
        power = jnp.floor(14.99 - jnp.log2(top))
        scaled = jnp.clip(jnp.round(both * jnp.exp2(power)), -32767.0, 32767.0)
        out[block, :rows, :] = scaled.astype(jnp.int32).astype(jnp.int16)
        power = jnp.broadcast_to(power, (out.shape[1] - rows, LANES))
        out[block, rows:, :] = power.astype(jnp.int32).astype(jnp.int16)


def finish_kernel(parts, virt, occ, out):
    rows = out.shape[0]
    size = rows * out.shape[1] // LANES
    summed = jnp.zeros((size, LANES), jnp.float32)
    for block in range(parts.shape[0]):
        power = parts[block, size:, :].astype(jnp.int32).astype(jnp.float32)
        value = parts[block, :size, :].astype(jnp.int32).astype(jnp.float32)
        summed += value * jnp.exp2(-power[0:1, :])
    for lane in range(out.shape[1] // LANES):
        ladder = summed[lane * rows : lane * rows + rows, :]
        denom = virt[lane : lane + 1, :] - occ[:rows, :]
        out[:, lane * LANES : lane * LANES + LANES] = ladder / denom


def on_device(amps, integrals, cd1, cd2, ab1, ab2, occ1, occ2, irrep, occ_energy, virt_energy):
    depth = amps.shape[1]
    width = integrals.shape[1]
    rows = occ1.shape[0]
    vmem = pl.BlockSpec(memory_space=pltpu.VMEM)
    smem = pl.BlockSpec(memory_space=pltpu.SMEM)
    square = lambda x: x.reshape(x.shape[0] // LANES, LANES)
    masked, virt, occ = pl.pallas_call(
        mask_kernel,
        out_shape=(
            pltpu.VMEM((depth, width), jnp.bfloat16),
            pltpu.VMEM((width // LANES, LANES), jnp.float32),
            pltpu.VMEM((16, LANES), jnp.float32),
        ),
        in_specs=[vmem] * 4 + [smem] * 2 + [vmem] * 2 + [smem, pl.BlockSpec(memory_space=pl.ANY)],
        out_specs=(vmem,) * 3,
        scratch_shapes=[pltpu.SemaphoreType.DMA((8,))],
        compiler_params=pltpu.CompilerParams(vmem_limit_bytes=4 * MIB),
    )(
        *[pltpu.with_memory_space_constraint(x, pltpu.HBM) for x in (
            square(cd1), square(cd2), square(ab1), square(ab2), occ1, occ2,
            irrep, virt_energy, occ_energy, integrals,
        )]
    )

    layer, core = lax.axis_index("z"), lax.axis_index("core")
    sign = (1 - 2 * (layer % 2)) * (1 - 2 * core)
    where = jnp.stack([layer, sign, core]).astype(jnp.int32)
    inner = lambda i: i ^ 1
    outer = lambda i: (i - 1 if i % 2 == 0 else i + 1) % 8
    odd, even = [], []
    for i in range(8):
        odd += [(2 * i, 2 * inner(i)), (2 * i + 1, 2 * outer(i) + 1)]
        even += [(2 * i, 2 * outer(i)), (2 * i + 1, 2 * inner(i) + 1)]
    axes = ("z", "core")
    a0, b0 = amps[:, : depth // 2], amps[:, depth // 2 :]
    a1 = jnp.concatenate([a0, lax.ppermute(a0, axes, odd)], axis=0)
    b1 = jnp.concatenate([b0, lax.ppermute(b0, axes, odd)], axis=0)
    b1, where = lax.optimization_barrier((b1, where))
    a2, b2 = lax.ppermute(a1, axes, even), lax.ppermute(b1, axes, even)
    a2, ready = lax.optimization_barrier((a2, virt))
    a3, b3 = lax.ppermute(a2, axes, odd), lax.ppermute(b2, axes, odd)
    a4, b4 = lax.ppermute(a3, axes, even), lax.ppermute(b3, axes, even)

    block = pltpu.VMEM((16, rows * width // LANES, LANES), jnp.float32)
    keep, send = pl.pallas_call(
        first_kernel,
        out_shape=(block, block),
        grid_spec=pltpu.PrefetchScalarGridSpec(
            num_scalar_prefetch=1,
            grid=(),
            in_specs=[vmem] * 8,
            out_specs=(vmem, vmem),
            scratch_shapes=[pltpu.VMEM((6 * amps.shape[0], width), jnp.float32)],
        ),
        compiler_params=pltpu.CompilerParams(vmem_limit_bytes=16 * MIB),
    )(where, ready, masked, a1, b1, a2, b2, a3, b3)
    keep, send = pl.pallas_call(
        last_kernel,
        out_shape=(block, block),
        grid_spec=pltpu.PrefetchScalarGridSpec(
            num_scalar_prefetch=1,
            grid=(),
            in_specs=[vmem] * 5,
            out_specs=(vmem, vmem),
            scratch_shapes=[pltpu.VMEM((2 * amps.shape[0], width), jnp.float32)],
        ),
        input_output_aliases={4: 0, 5: 1},
        compiler_params=pltpu.CompilerParams(vmem_limit_bytes=16 * MIB),
    )(where, masked, a4, b4, keep, send)

    got = lax.ppermute(send, "core", [(0, 1), (1, 0)])
    packed = pl.pallas_call(
        pack_kernel,
        out_shape=pltpu.VMEM((16, block.shape[1] + 16, LANES), jnp.int16),
        in_specs=[vmem] * 2,
        out_specs=vmem,
        compiler_params=pltpu.CompilerParams(vmem_limit_bytes=4 * MIB),
    )(keep, got)
    parts = lax.all_to_all(packed, ("y", "x"), 0, 0, tiled=True)
    return pl.pallas_call(
        finish_kernel,
        out_shape=jax.ShapeDtypeStruct((rows, width), jnp.float32),
        in_specs=[vmem] * 3,
        out_specs=vmem,
        compiler_params=pltpu.CompilerParams(vmem_limit_bytes=4 * MIB),
    )(parts, virt, occ)


def solution(mesh):
    fine = Mesh(mesh.devices.reshape(8, 4, 4, 2), ("z", "y", "x", "core"))
    col = ("y", "x", "core")
    in_specs = (
        P("z", col), P(col, "z"), P(col), P(col), P("z"), P("z"), P(col), P(col), P(), P(), P(),
    )
    return jax.shard_map(
        on_device, mesh=fine, in_specs=in_specs, out_specs=P(col, "z"), check_vma=False
    )
```

```python
import jax
import jax.numpy as jnp
from jax import lax
from jax.experimental import pallas as pl
from jax.experimental.pallas import tpu as pltpu
from jax.sharding import Mesh, PartitionSpec as P

LANES = 128
SHARDS = (0, -1, 1, -2, 2, -3, 3)
MIB = 1024 * 1024


def lookup(table_ref, index):
    size = table_ref.shape[0]
    high = index // LANES
    low = index % LANES
    picked = jnp.zeros(index.shape, table_ref.dtype)
    for row in range(-(-size // LANES)):
        line = table_ref[pl.ds(row * LANES, min(LANES, size - row * LANES))].reshape(1, -1)
        if line.shape[1] < LANES:
            line = jnp.pad(line, ((0, 0), (0, LANES - line.shape[1])))
        line = jnp.broadcast_to(line, index.shape)
        value = jnp.take_along_axis(line, low, axis=1, mode="promise_in_bounds")
        picked = jnp.where(high == row, value, picked)
    return picked


def mask_kernel(cd1, cd2, ab1, ab2, occ1, occ2, irrep, virt, energy, values, masked, virt_out, occ_out, arrived):
    blocks = arrived.shape[0]
    size = values.shape[0] // blocks
    copies = []
    for block in range(blocks):
        down = pl.ds(block * size, size)
        copies.append(
            pltpu.make_async_copy(values.at[down, :], masked.at[down, :], arrived.at[block])
        )
        copies[-1].start()

    virt_out[...] = lookup(virt, ab1[...]) + lookup(virt, ab2[...])
    for row in range(occ1.shape[0]):
        both = energy[occ1[row]] + energy[occ2[row]]
        occ_out[row : row + 1, :] = jnp.full((1, LANES), both, jnp.float32)
    label = lookup(irrep, ab1[...]) ^ lookup(irrep, ab2[...])
    other = label.astype(jnp.float32).astype(jnp.bfloat16)
    other = [jnp.broadcast_to(other[i : i + 1, :], (LANES, LANES)) for i in range(ab1.shape[0])]
    labels = []
    for tile in range(cd1.shape[0] // 8):
        part = slice(8 * tile, 8 * tile + 8)
        label = lookup(irrep, cd1[part, :]) ^ lookup(irrep, cd2[part, :])
        labels.append(label.astype(jnp.float32))

    for block in range(blocks):
        copies[block].wait()
        for part in range(block * size // LANES, (block + 1) * size // LANES):
            line = labels[part // 8][part % 8 : part % 8 + 1, :]
            label = jnp.broadcast_to(line, (LANES, LANES)).T.astype(jnp.bfloat16)
            down = slice(part * LANES, part * LANES + LANES)
            for lane in range(masked.shape[1] // LANES):
                across = slice(lane * LANES, lane * LANES + LANES)
                piece = masked[down, across]
                masked[down, across] = jnp.where(
                    label == other[lane], piece, jnp.zeros_like(piece)
                )


def spread(where, total, place, rows, keep, send):
    first_core = where[1] == 0
    for high in range(2):
        at = place * 4 * rows + 2 * high * rows
        even = total[at : at + rows, :]
        odd = total[at + rows : at + 2 * rows, :]
        kept = jnp.where(first_core, even, odd)
        sent = jnp.where(first_core, odd, even)
        for lane in range(kept.shape[1] // LANES):
            across = slice(lane * LANES, lane * LANES + LANES)
            down = slice(lane * rows, lane * rows + rows)
            keep[2 * place + high, down, :] = kept[:, across]
            send[2 * place + high, down, :] = sent[:, across]


def first_kernel(where, ready, masked, *refs):
    pieces = refs[:14]
    keep, send, total = refs[14:]
    half = masked.shape[0] // 2
    left = jnp.concatenate([piece[...] for piece in pieces[0::2]], axis=0)
    right = jnp.concatenate([piece[...] for piece in pieces[1::2]], axis=0)
    total[...] = jnp.dot(left, masked[:half, :], preferred_element_type=jnp.float32)
    total[...] += jnp.dot(right, masked[half:, :], preferred_element_type=jnp.float32)
    for place in range(7):
        spread(where, total, place, pieces[0].shape[0] // 4, keep, send)


def last_kernel(where, masked, left, right, keep, send, total):
    half = left.shape[1]
    total[...] = jnp.dot(left[...], masked[:half, :], preferred_element_type=jnp.float32)
    total[...] += jnp.dot(right[...], masked[half:, :], preferred_element_type=jnp.float32)
    spread(where, total, 0, left.shape[0] // 4, keep, send)


def pack_kernel(where, keep, got, last_keep, last_got, out):
    rows = keep.shape[1]
    for place, shift in enumerate(SHARDS + (4,)):
        shard = lax.rem(where[0] + (shift + 8), 8)
        for high in range(2):
            if place < len(SHARDS):
                both = keep[2 * place + high] + got[2 * place + high]
            else:
                both = last_keep[high] + last_got[high]
            top = jnp.maximum(jnp.max(jnp.abs(both), axis=0, keepdims=True), 1e-30)
            power = jnp.floor(14.99 - jnp.log2(top))
            scaled = jnp.clip(jnp.round(both * jnp.exp2(power)), -32767.0, 32767.0)
            out[2 * shard + high, :rows, :] = scaled.astype(jnp.int32).astype(jnp.int16)
            power = jnp.broadcast_to(power, (out.shape[1] - rows, LANES))
            out[2 * shard + high, rows:, :] = power.astype(jnp.int32).astype(jnp.int16)


def finish_kernel(parts, virt, occ, out):
    rows = out.shape[0]
    size = rows * out.shape[1] // LANES
    summed = jnp.zeros((size, LANES), jnp.float32)
    for block in range(parts.shape[0]):
        power = parts[block, size:, :].astype(jnp.int32).astype(jnp.float32)
        value = parts[block, :size, :].astype(jnp.int32).astype(jnp.float32)
        summed += value * jnp.exp2(-power[0:1, :])
    for lane in range(out.shape[1] // LANES):
        ladder = summed[lane * rows : lane * rows + rows, :]
        denom = virt[lane : lane + 1, :] - occ[:rows, :]
        out[:, lane * LANES : lane * LANES + LANES] = ladder / denom


def on_device(amps, integrals, cd1, cd2, ab1, ab2, occ1, occ2, irrep, occ_energy, virt_energy):
    depth = amps.shape[1]
    width = integrals.shape[1]
    rows = occ1.shape[0]
    vmem = pl.BlockSpec(memory_space=pltpu.VMEM)
    smem = pl.BlockSpec(memory_space=pltpu.SMEM)
    square = lambda x: x.reshape(x.shape[0] // LANES, LANES)
    masked, virt, occ = pl.pallas_call(
        mask_kernel,
        out_shape=(
            pltpu.VMEM((depth, width), jnp.bfloat16),
            pltpu.VMEM((width // LANES, LANES), jnp.float32),
            pltpu.VMEM((16, LANES), jnp.float32),
        ),
        in_specs=[vmem] * 4 + [smem] * 2 + [vmem] * 2 + [smem, pl.BlockSpec(memory_space=pl.ANY)],
        out_specs=(vmem,) * 3,
        scratch_shapes=[pltpu.SemaphoreType.DMA((8,))],
        compiler_params=pltpu.CompilerParams(vmem_limit_bytes=4 * MIB),
    )(
        *[pltpu.with_memory_space_constraint(x, pltpu.HBM) for x in (
            square(cd1), square(cd2), square(ab1), square(ab2), occ1, occ2,
            irrep, virt_energy, occ_energy, integrals,
        )]
    )

    where = jnp.stack([lax.axis_index("z"), lax.axis_index("core")]).astype(jnp.int32)
    forward = [(i, (i + 1) % 8) for i in range(8)]
    backward = [(i, (i - 1) % 8) for i in range(8)]
    up = [amps[:, : depth // 2], amps[:, depth // 2 :]]
    down = list(up)
    pieces = list(up)
    for hop in range(3):
        up[0] = lax.ppermute(up[0], "z", forward)
        up[1] = lax.ppermute(up[1], "z", forward)
        down[0] = lax.ppermute(down[0], "z", backward)
        down[1] = lax.ppermute(down[1], "z", backward)
        if hop == 0:
            up[0], ready, where = lax.optimization_barrier((up[0], virt, where))
        pieces += up + down
    last = [lax.ppermute(up[0], "z", forward), lax.ppermute(down[1], "z", backward)]
    size = rows * width // LANES
    first = pltpu.VMEM((14, size, LANES), jnp.float32)
    final = pltpu.VMEM((2, size, LANES), jnp.float32)
    keep, send = pl.pallas_call(
        first_kernel,
        out_shape=(first, first),
        grid_spec=pltpu.PrefetchScalarGridSpec(
            num_scalar_prefetch=1,
            grid=(),
            in_specs=[vmem] * 16,
            out_specs=(vmem, vmem),
            scratch_shapes=[pltpu.VMEM((7 * amps.shape[0], width), jnp.float32)],
        ),
        compiler_params=pltpu.CompilerParams(vmem_limit_bytes=8 * MIB),
    )(where, ready, masked, *pieces)
    swap = [(0, 1), (1, 0)]
    send, *last = lax.optimization_barrier((send, *last))
    got = lax.ppermute(send, "core", swap)
    last_keep, last_send = pl.pallas_call(
        last_kernel,
        out_shape=(final, final),
        grid_spec=pltpu.PrefetchScalarGridSpec(
            num_scalar_prefetch=1,
            grid=(),
            in_specs=[vmem] * 3,
            out_specs=(vmem, vmem),
            scratch_shapes=[pltpu.VMEM((amps.shape[0], width), jnp.float32)],
        ),
        compiler_params=pltpu.CompilerParams(vmem_limit_bytes=8 * MIB),
    )(where, masked, *last)
    last_got = lax.ppermute(last_send, "core", swap)
    packed = pl.pallas_call(
        pack_kernel,
        out_shape=pltpu.VMEM((16, size + 16, LANES), jnp.int16),
        grid_spec=pltpu.PrefetchScalarGridSpec(
            num_scalar_prefetch=1, grid=(), in_specs=[vmem] * 4, out_specs=vmem
        ),
        compiler_params=pltpu.CompilerParams(vmem_limit_bytes=4 * MIB),
    )(where, keep, got, last_keep, last_got)
    parts = lax.all_to_all(packed, ("y", "x"), 0, 0, tiled=True)
    return pl.pallas_call(
        finish_kernel,
        out_shape=jax.ShapeDtypeStruct((rows, width), jnp.float32),
        in_specs=[vmem] * 3,
        out_specs=vmem,
        compiler_params=pltpu.CompilerParams(vmem_limit_bytes=4 * MIB),
    )(parts, virt, occ)


def solution(mesh):
    fine = Mesh(mesh.devices.reshape(8, 4, 4, 2), ("z", "y", "x", "core"))
    col = ("y", "x", "core")
    in_specs = (
        P("z", col), P(col, "z"), P(col), P(col), P("z"), P("z"), P(col), P(col), P(), P(), P(),
    )
    return jax.shard_map(
        on_device, mesh=fine, in_specs=in_specs, out_specs=P(col, "z"), check_vma=False
    )
```

```python
import jax
import jax.numpy as jnp
from jax import lax
from jax.experimental import pallas as pl
from jax.experimental.pallas import tpu as pltpu
from jax.sharding import Mesh, PartitionSpec as P

LANES = 128
SHARDS = (0, -1, 1, -2, 2, -3, 3, 4)
MIB = 1024 * 1024


def lookup(table_ref, index):
    size = table_ref.shape[0]
    high = index // LANES
    low = index % LANES
    picked = jnp.zeros(index.shape, table_ref.dtype)
    for row in range(-(-size // LANES)):
        line = table_ref[pl.ds(row * LANES, min(LANES, size - row * LANES))].reshape(1, -1)
        if line.shape[1] < LANES:
            line = jnp.pad(line, ((0, 0), (0, LANES - line.shape[1])))
        line = jnp.broadcast_to(line, index.shape)
        value = jnp.take_along_axis(line, low, axis=1, mode="promise_in_bounds")
        picked = jnp.where(high == row, value, picked)
    return picked


def mask_kernel(cd1, cd2, ab1, ab2, occ1, occ2, irrep, virt, energy, values, masked, virt_out, occ_out, arrived):
    blocks = arrived.shape[0]
    size = values.shape[0] // blocks
    copies = []
    for block in range(blocks):
        down = pl.ds(block * size, size)
        copies.append(
            pltpu.make_async_copy(values.at[down, :], masked.at[down, :], arrived.at[block])
        )
        copies[-1].start()

    virt_out[...] = lookup(virt, ab1[...]) + lookup(virt, ab2[...])
    for row in range(occ1.shape[0]):
        both = energy[occ1[row]] + energy[occ2[row]]
        occ_out[row : row + 1, :] = jnp.full((1, LANES), both, jnp.float32)
    label = lookup(irrep, ab1[...]) ^ lookup(irrep, ab2[...])
    other = label.astype(jnp.float32).astype(jnp.bfloat16)
    other = [jnp.broadcast_to(other[i : i + 1, :], (LANES, LANES)) for i in range(ab1.shape[0])]
    labels = []
    for tile in range(cd1.shape[0] // 8):
        part = slice(8 * tile, 8 * tile + 8)
        label = lookup(irrep, cd1[part, :]) ^ lookup(irrep, cd2[part, :])
        labels.append(label.astype(jnp.float32))

    for block in range(blocks):
        copies[block].wait()
        for part in range(block * size // LANES, (block + 1) * size // LANES):
            line = labels[part // 8][part % 8 : part % 8 + 1, :]
            label = jnp.broadcast_to(line, (LANES, LANES)).T.astype(jnp.bfloat16)
            down = slice(part * LANES, part * LANES + LANES)
            for lane in range(masked.shape[1] // LANES):
                across = slice(lane * LANES, lane * LANES + LANES)
                piece = masked[down, across]
                masked[down, across] = jnp.where(
                    label == other[lane], piece, jnp.zeros_like(piece)
                )


def spread(where, total, place, rows, keep, send):
    first_core = where[1] == 0
    for high in range(2):
        at = place * 4 * rows + 2 * high * rows
        even = total[at : at + rows, :]
        odd = total[at + rows : at + 2 * rows, :]
        kept = jnp.where(first_core, even, odd)
        sent = jnp.where(first_core, odd, even)
        for lane in range(kept.shape[1] // LANES):
            across = slice(lane * LANES, lane * LANES + LANES)
            down = slice(lane * rows, lane * rows + rows)
            keep[2 * place + high, down, :] = kept[:, across]
            send[2 * place + high, down, :] = sent[:, across]


def ladder_kernel(where, ready, masked, *refs):
    pieces = refs[:-3]
    keep, send, total = refs[-3:]
    half = masked.shape[0] // 2
    left = jnp.concatenate([piece[...] for piece in pieces[0::2]], axis=0)
    right = jnp.concatenate([piece[...] for piece in pieces[1::2]], axis=0)
    total[...] = jnp.dot(left, masked[:half, :], preferred_element_type=jnp.float32)
    total[...] += jnp.dot(right, masked[half:, :], preferred_element_type=jnp.float32)
    for place in range(len(pieces) // 2):
        spread(where, total, place, pieces[0].shape[0] // 4, keep, send)


def ladder(where, ready, masked, pieces):
    vmem = pl.BlockSpec(memory_space=pltpu.VMEM)
    count = len(pieces) // 2
    height, width = pieces[0].shape[0], masked.shape[1]
    block = pltpu.VMEM((2 * count, height * width // 4 // LANES, LANES), jnp.float32)
    return pl.pallas_call(
        ladder_kernel,
        out_shape=(block, block),
        grid_spec=pltpu.PrefetchScalarGridSpec(
            num_scalar_prefetch=1,
            grid=(),
            in_specs=[vmem] * (2 + len(pieces)),
            out_specs=(vmem, vmem),
            scratch_shapes=[pltpu.VMEM((count * height, width), jnp.float32)],
        ),
        compiler_params=pltpu.CompilerParams(vmem_limit_bytes=8 * MIB),
    )(where, ready, masked, *pieces)


def pack_kernel(where, *refs):
    out = refs[-1]
    kept, got = refs[: len(refs) // 2], refs[len(refs) // 2 : -1]
    rows = kept[0].shape[1]
    shifts = iter(SHARDS)
    for mine, other in zip(kept, got):
        for place in range(mine.shape[0] // 2):
            shard = lax.rem(where[0] + (next(shifts) + 8), 8)
            for high in range(2):
                both = mine[2 * place + high] + other[2 * place + high]
                top = jnp.maximum(jnp.max(jnp.abs(both), axis=0, keepdims=True), 1e-30)
                power = jnp.floor(14.99 - jnp.log2(top))
                scaled = jnp.clip(jnp.round(both * jnp.exp2(power)), -32767.0, 32767.0)
                out[2 * shard + high, :rows, :] = scaled.astype(jnp.int32).astype(jnp.int16)
                power = jnp.broadcast_to(power, (out.shape[1] - rows, LANES))
                out[2 * shard + high, rows:, :] = power.astype(jnp.int32).astype(jnp.int16)


def finish_kernel(parts, virt, occ, out):
    rows = out.shape[0]
    size = rows * out.shape[1] // LANES
    summed = jnp.zeros((size, LANES), jnp.float32)
    for block in range(parts.shape[0]):
        power = parts[block, size:, :].astype(jnp.int32).astype(jnp.float32)
        value = parts[block, :size, :].astype(jnp.int32).astype(jnp.float32)
        summed += value * jnp.exp2(-power[0:1, :])
    for lane in range(out.shape[1] // LANES):
        ladder = summed[lane * rows : lane * rows + rows, :]
        denom = virt[lane : lane + 1, :] - occ[:rows, :]
        out[:, lane * LANES : lane * LANES + LANES] = ladder / denom


def on_device(amps, integrals, cd1, cd2, ab1, ab2, occ1, occ2, irrep, occ_energy, virt_energy):
    depth = amps.shape[1]
    width = integrals.shape[1]
    rows = occ1.shape[0]
    vmem = pl.BlockSpec(memory_space=pltpu.VMEM)
    smem = pl.BlockSpec(memory_space=pltpu.SMEM)
    square = lambda x: x.reshape(x.shape[0] // LANES, LANES)
    masked, virt, occ = pl.pallas_call(
        mask_kernel,
        out_shape=(
            pltpu.VMEM((depth, width), jnp.bfloat16),
            pltpu.VMEM((width // LANES, LANES), jnp.float32),
            pltpu.VMEM((16, LANES), jnp.float32),
        ),
        in_specs=[vmem] * 4 + [smem] * 2 + [vmem] * 2 + [smem, pl.BlockSpec(memory_space=pl.ANY)],
        out_specs=(vmem,) * 3,
        scratch_shapes=[pltpu.SemaphoreType.DMA((8,))],
        compiler_params=pltpu.CompilerParams(vmem_limit_bytes=4 * MIB),
    )(
        *[pltpu.with_memory_space_constraint(x, pltpu.HBM) for x in (
            square(cd1), square(cd2), square(ab1), square(ab2), occ1, occ2,
            irrep, virt_energy, occ_energy, integrals,
        )]
    )

    where = jnp.stack([lax.axis_index("z"), lax.axis_index("core")]).astype(jnp.int32)
    forward = [(i, (i + 1) % 8) for i in range(8)]
    backward = [(i, (i - 1) % 8) for i in range(8)]
    up = [amps[:, : depth // 2], amps[:, depth // 2 :]]
    down = list(up)
    pieces = list(up)
    for hop in range(3):
        up[0] = lax.ppermute(up[0], "z", forward)
        up[1] = lax.ppermute(up[1], "z", forward)
        down[0] = lax.ppermute(down[0], "z", backward)
        down[1] = lax.ppermute(down[1], "z", backward)
        if hop == 0:
            up[0], ready, where = lax.optimization_barrier((up[0], virt, where))
        pieces += up + down
    ready, up[0], down[1] = lax.optimization_barrier((ready, up[0], down[1]))
    last = [lax.ppermute(up[0], "z", forward), lax.ppermute(down[1], "z", backward)]
    swap = [(0, 1), (1, 0)]
    keep1, send1 = ladder(where, ready, masked, pieces[:10])
    keep2, send2 = ladder(where, ready, masked, pieces[10:])
    send1, send2, *last = lax.optimization_barrier((send1, send2, *last))
    got1, got2 = lax.ppermute(send1, "core", swap), lax.ppermute(send2, "core", swap)
    keep3, send3 = ladder(where, ready, masked, last)
    got3 = lax.ppermute(send3, "core", swap)
    packed = pl.pallas_call(
        pack_kernel,
        out_shape=pltpu.VMEM((16, rows * width // LANES + 16, LANES), jnp.int16),
        grid_spec=pltpu.PrefetchScalarGridSpec(
            num_scalar_prefetch=1, grid=(), in_specs=[vmem] * 6, out_specs=vmem
        ),
        compiler_params=pltpu.CompilerParams(vmem_limit_bytes=4 * MIB),
    )(where, keep1, keep2, keep3, got1, got2, got3)
    parts = lax.all_to_all(packed, ("y", "x"), 0, 0, tiled=True)
    return pl.pallas_call(
        finish_kernel,
        out_shape=jax.ShapeDtypeStruct((rows, width), jnp.float32),
        in_specs=[vmem] * 3,
        out_specs=vmem,
        compiler_params=pltpu.CompilerParams(vmem_limit_bytes=4 * MIB),
    )(parts, virt, occ)


def solution(mesh):
    fine = Mesh(mesh.devices.reshape(8, 4, 4, 2), ("z", "y", "x", "core"))
    col = ("y", "x", "core")
    in_specs = (
        P("z", col), P(col, "z"), P(col), P(col), P("z"), P("z"), P(col), P(col), P(), P(), P(),
    )
    return jax.shard_map(
        on_device, mesh=fine, in_specs=in_specs, out_specs=P(col, "z"), check_vma=False
    )
```

```python
import jax
import jax.numpy as jnp
from jax import lax
from jax.experimental import pallas as pl
from jax.experimental.pallas import tpu as pltpu
from jax.sharding import Mesh, PartitionSpec as P

LANES = 128
SHARDS = (0, -1, 1, -2, 2, -3, 3)
MIB = 1024 * 1024


def lookup(table_ref, index):
    size = table_ref.shape[0]
    high = index // LANES
    low = index % LANES
    picked = jnp.zeros(index.shape, table_ref.dtype)
    for row in range(-(-size // LANES)):
        line = table_ref[pl.ds(row * LANES, min(LANES, size - row * LANES))].reshape(1, -1)
        if line.shape[1] < LANES:
            line = jnp.pad(line, ((0, 0), (0, LANES - line.shape[1])))
        line = jnp.broadcast_to(line, index.shape)
        value = jnp.take_along_axis(line, low, axis=1, mode="promise_in_bounds")
        picked = jnp.where(high == row, value, picked)
    return picked


def mask_kernel(*refs):
    values = refs[9]
    masked, virt_out, occ_out = refs[10:13]
    cd1, cd2, ab1, ab2, occ1, occ2, irrep, virt, energy = refs[13:22]
    ready, arrived = refs[22:]
    small = [
        pltpu.make_async_copy(refs[i], refs[13 + i], ready.at[i]) for i in range(9)
    ]
    blocks = arrived.shape[0]
    size = values.shape[0] // blocks
    copies = []
    for block in range(blocks):
        down = pl.ds(block * size, size)
        copies.append(
            pltpu.make_async_copy(values.at[down, :], masked.at[down, :], arrived.at[block])
        )
    for copy in small + copies:
        copy.start()
    for copy in small:
        copy.wait()

    label = lookup(irrep, ab1[...]) ^ lookup(irrep, ab2[...])
    other = label.astype(jnp.float32).astype(jnp.bfloat16)
    other = [jnp.broadcast_to(other[i : i + 1, :], (LANES, LANES)) for i in range(ab1.shape[0])]
    labels = []
    for tile in range(cd1.shape[0] // 8):
        part = slice(8 * tile, 8 * tile + 8)
        label = lookup(irrep, cd1[part, :]) ^ lookup(irrep, cd2[part, :])
        labels.append(label.astype(jnp.float32))
    virt_out[...] = lookup(virt, ab1[...]) + lookup(virt, ab2[...])
    both = jnp.zeros((8, LANES), jnp.float32)
    for occ in (occ1, occ2):
        row = occ[...].reshape(1, -1)
        row = jnp.pad(row, ((0, 0), (0, LANES - row.shape[1])))
        both += lookup(energy, jnp.broadcast_to(row, (8, LANES)))
    column = jnp.broadcast_to(both[0:1, :], (LANES, LANES)).T
    occ_out[...] = column[: occ_out.shape[0], :]

    for block in range(blocks):
        copies[block].wait()
        for part in range(block * size // LANES, (block + 1) * size // LANES):
            line = labels[part // 8][part % 8 : part % 8 + 1, :]
            label = jnp.broadcast_to(line, (LANES, LANES)).T.astype(jnp.bfloat16)
            down = slice(part * LANES, part * LANES + LANES)
            for lane in range(masked.shape[1] // LANES):
                across = slice(lane * LANES, lane * LANES + LANES)
                piece = masked[down, across]
                masked[down, across] = jnp.where(
                    label == other[lane], piece, jnp.zeros_like(piece)
                )


def spread(where, total, place, rows, keep, send):
    first_core = where[1] == 0
    for high in range(2):
        at = place * 4 * rows + 2 * high * rows
        even = total[at : at + rows, :]
        odd = total[at + rows : at + 2 * rows, :]
        kept = jnp.where(first_core, even, odd)
        sent = jnp.where(first_core, odd, even)
        for lane in range(kept.shape[1] // LANES):
            across = slice(lane * LANES, lane * LANES + LANES)
            down = slice(lane * rows, lane * rows + rows)
            keep[2 * place + high, down, :] = kept[:, across]
            send[2 * place + high, down, :] = sent[:, across]


def ladder_kernel(where, ready, masked, *refs):
    pieces = refs[:-3]
    keep, send, total = refs[-3:]
    left = jnp.concatenate([piece[...] for piece in pieces[0::2]], axis=0)
    right = jnp.concatenate([piece[...] for piece in pieces[1::2]], axis=0)
    total[...] = jnp.dot(
        jnp.concatenate([left, right], axis=1), masked[...], preferred_element_type=jnp.float32
    )
    for place in range(len(pieces) // 2):
        spread(where, total, place, pieces[0].shape[0] // 4, keep, send)


def ladder(where, ready, masked, pieces):
    vmem = pl.BlockSpec(memory_space=pltpu.VMEM)
    count = len(pieces) // 2
    height, width = pieces[0].shape[0], masked.shape[1]
    block = pltpu.VMEM((2 * count, height * width // 4 // LANES, LANES), jnp.float32)
    return pl.pallas_call(
        ladder_kernel,
        out_shape=(block, block),
        grid_spec=pltpu.PrefetchScalarGridSpec(
            num_scalar_prefetch=1,
            grid=(),
            in_specs=[vmem] * (2 + len(pieces)),
            out_specs=(vmem, vmem),
            scratch_shapes=[pltpu.VMEM((count * height, width), jnp.float32)],
        ),
        compiler_params=pltpu.CompilerParams(vmem_limit_bytes=10 * MIB),
    )(where, ready, masked, *pieces)


def pack_into(where, out, kept, got, shifts):
    rows = kept.shape[1]
    for place, shift in enumerate(shifts):
        shard = lax.rem(where[0] + (shift + 8), 8)
        for high in range(2):
            both = kept[2 * place + high] + got[2 * place + high]
            top = jnp.maximum(jnp.max(jnp.abs(both), axis=0, keepdims=True), 1e-30)
            power = jnp.floor(14.99 - jnp.log2(top))
            scaled = jnp.clip(jnp.round(both * jnp.exp2(power)), -32767.0, 32767.0)
            out[2 * shard + high, :rows, :] = scaled.astype(jnp.int32).astype(jnp.int16)
            power = jnp.broadcast_to(power, (out.shape[1] - rows, LANES))
            out[2 * shard + high, rows:, :] = power.astype(jnp.int32).astype(jnp.int16)


def pack_kernel(where, kept, got, out):
    for high in range(2):
        out[2 * lax.rem(where[0] + 4, 8) + high] = jnp.zeros(out.shape[1:], jnp.int16)
    pack_into(where, out, kept, got, SHARDS)


def repack_kernel(where, kept, got, packed, out):
    out[...] = packed[...]
    pack_into(where, out, kept, got, (4,))


def finish_kernel(parts, virt, occ, out):
    rows = out.shape[0]
    size = rows * out.shape[1] // LANES
    summed = jnp.zeros((size, LANES), jnp.float32)
    for block in range(parts.shape[0]):
        power = parts[block, size:, :].astype(jnp.int32).astype(jnp.float32)
        value = parts[block, :size, :].astype(jnp.int32).astype(jnp.float32)
        summed += value * jnp.exp2(-power[0:1, :])
    for lane in range(out.shape[1] // LANES):
        ladder = summed[lane * rows : lane * rows + rows, :]
        denom = virt[lane : lane + 1, :] - occ[:rows, :]
        out[:, lane * LANES : lane * LANES + LANES] = ladder / denom


def on_device(amps, integrals, cd1, cd2, ab1, ab2, occ1, occ2, irrep, occ_energy, virt_energy):
    depth = amps.shape[1]
    width = integrals.shape[1]
    rows = occ1.shape[0]
    vmem = pl.BlockSpec(memory_space=pltpu.VMEM)
    square = lambda x: x.reshape(x.shape[0] // LANES, LANES)
    small = [square(x) for x in (cd1, cd2, ab1, ab2)] + [occ1, occ2, irrep, virt_energy, occ_energy]
    masked, virt, occ = pl.pallas_call(
        mask_kernel,
        out_shape=(
            pltpu.VMEM((depth, width), jnp.bfloat16),
            pltpu.VMEM((width // LANES, LANES), jnp.float32),
            pltpu.VMEM((16, LANES), jnp.float32),
        ),
        in_specs=[pl.BlockSpec(memory_space=pl.ANY)] * 10,
        out_specs=(vmem,) * 3,
        scratch_shapes=[
            pltpu.VMEM(x.shape, x.dtype) for x in small
        ] + [pltpu.SemaphoreType.DMA((9,)), pltpu.SemaphoreType.DMA((8,))],
        compiler_params=pltpu.CompilerParams(vmem_limit_bytes=4 * MIB),
    )(
        *[pltpu.with_memory_space_constraint(x, pltpu.HBM) for x in small + [integrals]]
    )

    where = jnp.stack([lax.axis_index("z"), lax.axis_index("core")]).astype(jnp.int32)
    forward = [(i, (i + 1) % 8) for i in range(8)]
    backward = [(i, (i - 1) % 8) for i in range(8)]
    again = lax.optimization_barrier(amps)
    up = [amps[:, : depth // 2], again[:, depth // 2 :]]
    down = list(up)
    pieces = list(up)
    for hop in range(3):
        up[0] = lax.ppermute(up[0], "z", forward)
        up[1] = lax.ppermute(up[1], "z", forward)
        down[0] = lax.ppermute(down[0], "z", backward)
        down[1] = lax.ppermute(down[1], "z", backward)
        if hop == 0:
            up[0], ready, where = lax.optimization_barrier((up[0], virt, where))
        pieces += up + down
    last = [lax.ppermute(up[0], "z", forward), lax.ppermute(down[1], "z", backward)]
    swap = [(0, 1), (1, 0)]
    keep, send = ladder(where, ready, masked, pieces)
    send, *last = lax.optimization_barrier((send, *last))
    got = lax.ppermute(send, "core", swap)
    last_keep, last_send = ladder(where, ready, masked, last)
    last_got = lax.ppermute(last_send, "core", swap)
    whole = pltpu.VMEM((16, rows * width // LANES + 16, LANES), jnp.int16)
    pack = lambda kernel, aliases, *operands: pl.pallas_call(
        kernel,
        out_shape=whole,
        grid_spec=pltpu.PrefetchScalarGridSpec(
            num_scalar_prefetch=1, grid=(), in_specs=[vmem] * (len(operands) - 1), out_specs=vmem
        ),
        input_output_aliases=aliases,
        compiler_params=pltpu.CompilerParams(vmem_limit_bytes=4 * MIB),
    )(*operands)
    packed = pack(pack_kernel, {}, where, keep, got)
    packed = pack(repack_kernel, {3: 0}, where, last_keep, last_got, packed)
    parts = lax.all_to_all(packed, ("y", "x"), 0, 0, tiled=True)
    return pl.pallas_call(
        finish_kernel,
        out_shape=jax.ShapeDtypeStruct((rows, width), jnp.float32),
        in_specs=[vmem] * 3,
        out_specs=vmem,
        compiler_params=pltpu.CompilerParams(vmem_limit_bytes=4 * MIB),
    )(parts, virt, occ)


def solution(mesh):
    fine = Mesh(mesh.devices.reshape(8, 4, 4, 2), ("z", "y", "x", "core"))
    col = ("y", "x", "core")
    in_specs = (
        P("z", col), P(col, "z"), P(col), P(col), P("z"), P("z"), P(col), P(col), P(), P(), P(),
    )
    return jax.shard_map(
        on_device, mesh=fine, in_specs=in_specs, out_specs=P(col, "z"), check_vma=False
    )
```

```python
import jax
import jax.numpy as jnp
from jax import lax
from jax.experimental import pallas as pl
from jax.experimental.pallas import tpu as pltpu
from jax.sharding import Mesh, PartitionSpec as P

LANES = 128
SHARDS = (0, -1, 1, -2, 2, -3, 3)
MIB = 1024 * 1024


def lookup(table_ref, index):
    size = table_ref.shape[0]
    high = index // LANES
    low = index % LANES
    picked = jnp.zeros(index.shape, table_ref.dtype)
    for row in range(-(-size // LANES)):
        line = table_ref[pl.ds(row * LANES, min(LANES, size - row * LANES))].reshape(1, -1)
        if line.shape[1] < LANES:
            line = jnp.pad(line, ((0, 0), (0, LANES - line.shape[1])))
        line = jnp.broadcast_to(line, index.shape)
        value = jnp.take_along_axis(line, low, axis=1, mode="promise_in_bounds")
        picked = jnp.where(high == row, value, picked)
    return picked


def fetch(values, masked, arrived, first):
    blocks = arrived.shape[0]
    size = masked.shape[0] // blocks
    copies = []
    for block in range(blocks):
        copies.append(
            pltpu.make_async_copy(
                values.at[pl.ds(first + block * size, size), :],
                masked.at[pl.ds(block * size, size), :],
                arrived.at[block],
            )
        )
        copies[-1].start()
    return copies


def apply_mask(copies, masked, lines, other):
    size = masked.shape[0] // len(copies)
    other = [jnp.broadcast_to(other[i : i + 1, :], (LANES, LANES)) for i in range(other.shape[0])]
    for block, copy in enumerate(copies):
        copy.wait()
        for part in range(block * size // LANES, (block + 1) * size // LANES):
            label = jnp.broadcast_to(lines(part), (LANES, LANES)).T.astype(jnp.bfloat16)
            down = slice(part * LANES, part * LANES + LANES)
            for lane in range(masked.shape[1] // LANES):
                across = slice(lane * LANES, lane * LANES + LANES)
                piece = masked[down, across]
                masked[down, across] = jnp.where(
                    label == other[lane], piece, jnp.zeros_like(piece)
                )


def low_kernel(cd1, cd2, ab1, ab2, occ1, occ2, irrep, virt, energy, values, masked, cd_out, ab_out, virt_out, occ_out, arrived):
    copies = fetch(values, masked, arrived, 0)
    label = lookup(irrep, ab1[...]) ^ lookup(irrep, ab2[...])
    other = label.astype(jnp.float32)
    ab_out[...] = other
    labels = []
    for tile in range(cd1.shape[0] // 8):
        part = slice(8 * tile, 8 * tile + 8)
        label = lookup(irrep, cd1[part, :]) ^ lookup(irrep, cd2[part, :])
        labels.append(label.astype(jnp.float32))
    for tile in range(len(labels) // 2):
        cd_out[8 * tile : 8 * tile + 8, :] = labels[len(labels) // 2 + tile]
    virt_out[...] = lookup(virt, ab1[...]) + lookup(virt, ab2[...])
    for row in range(occ1.shape[0]):
        both = energy[occ1[row]] + energy[occ2[row]]
        occ_out[row : row + 1, :] = jnp.full((1, LANES), both, jnp.float32)
    lines = lambda part: labels[part // 8][part % 8 : part % 8 + 1, :]
    apply_mask(copies, masked, lines, other.astype(jnp.bfloat16))


def high_kernel(cd, ab, values, after1, after2, masked, ready, arrived):
    copies = fetch(values, masked, arrived, masked.shape[0])
    ready[...] = ab[...]
    lines = lambda part: cd[part : part + 1, :]
    apply_mask(copies, masked, lines, ab[...].astype(jnp.bfloat16))


def spread(where, total, place, rows, keep, send):
    first_core = where[1] == 0
    for high in range(2):
        at = place * 4 * rows + 2 * high * rows
        even = total[at : at + rows, :]
        odd = total[at + rows : at + 2 * rows, :]
        kept = jnp.where(first_core, even, odd)
        sent = jnp.where(first_core, odd, even)
        for lane in range(kept.shape[1] // LANES):
            across = slice(lane * LANES, lane * LANES + LANES)
            down = slice(lane * rows, lane * rows + rows)
            keep[2 * place + high, down, :] = kept[:, across]
            send[2 * place + high, down, :] = sent[:, across]


def first_kernel(where, ready, low, high, *refs):
    pieces = refs[:14]
    keep, send, total = refs[14:]
    left = jnp.concatenate([piece[...] for piece in pieces[0::2]], axis=0)
    right = jnp.concatenate([piece[...] for piece in pieces[1::2]], axis=0)
    total[...] = jnp.dot(left, low[...], preferred_element_type=jnp.float32)
    total[...] += jnp.dot(right, high[...], preferred_element_type=jnp.float32)
    for place in range(7):
        spread(where, total, place, pieces[0].shape[0] // 4, keep, send)


def last_kernel(where, low, high, left, right, keep, send, total):
    total[...] = jnp.dot(left[...], low[...], preferred_element_type=jnp.float32)
    total[...] += jnp.dot(right[...], high[...], preferred_element_type=jnp.float32)
    spread(where, total, 0, left.shape[0] // 4, keep, send)


def pack_kernel(where, keep, got, last_keep, last_got, out):
    rows = keep.shape[1]
    for place, shift in enumerate(SHARDS + (4,)):
        shard = lax.rem(where[0] + (shift + 8), 8)
        for high in range(2):
            if place < len(SHARDS):
                both = keep[2 * place + high] + got[2 * place + high]
            else:
                both = last_keep[high] + last_got[high]
            top = jnp.maximum(jnp.max(jnp.abs(both), axis=0, keepdims=True), 1e-30)
            power = jnp.floor(14.99 - jnp.log2(top))
            scaled = jnp.clip(jnp.round(both * jnp.exp2(power)), -32767.0, 32767.0)
            out[2 * shard + high, :rows, :] = scaled.astype(jnp.int32).astype(jnp.int16)
            power = jnp.broadcast_to(power, (out.shape[1] - rows, LANES))
            out[2 * shard + high, rows:, :] = power.astype(jnp.int32).astype(jnp.int16)


def finish_kernel(parts, virt, occ, out):
    rows = out.shape[0]
    size = rows * out.shape[1] // LANES
    summed = jnp.zeros((size, LANES), jnp.float32)
    for block in range(parts.shape[0]):
        power = parts[block, size:, :].astype(jnp.int32).astype(jnp.float32)
        value = parts[block, :size, :].astype(jnp.int32).astype(jnp.float32)
        summed += value * jnp.exp2(-power[0:1, :])
    for lane in range(out.shape[1] // LANES):
        ladder = summed[lane * rows : lane * rows + rows, :]
        denom = virt[lane : lane + 1, :] - occ[:rows, :]
        out[:, lane * LANES : lane * LANES + LANES] = ladder / denom


def on_device(amps, integrals, cd1, cd2, ab1, ab2, occ1, occ2, irrep, occ_energy, virt_energy):
    depth = amps.shape[1]
    width = integrals.shape[1]
    rows = occ1.shape[0]
    vmem = pl.BlockSpec(memory_space=pltpu.VMEM)
    smem = pl.BlockSpec(memory_space=pltpu.SMEM)
    square = lambda x: x.reshape(x.shape[0] // LANES, LANES)
    tables = [pltpu.with_memory_space_constraint(x, pltpu.HBM) for x in (
        square(cd1), square(cd2), square(ab1), square(ab2), occ1, occ2,
        irrep, virt_energy, occ_energy, integrals,
    )]
    half = pltpu.VMEM((depth // 2, width), jnp.bfloat16)
    lines = pltpu.VMEM((width // LANES, LANES), jnp.float32)
    hbm = pl.BlockSpec(memory_space=pl.ANY)
    low, cd, ab, virt, occ = pl.pallas_call(
        low_kernel,
        out_shape=(
            half,
            pltpu.VMEM((depth // LANES // 2, LANES), jnp.float32),
            lines,
            lines,
            pltpu.VMEM((16, LANES), jnp.float32),
        ),
        in_specs=[vmem] * 4 + [smem] * 2 + [vmem] * 2 + [smem, hbm],
        out_specs=(vmem,) * 5,
        scratch_shapes=[pltpu.SemaphoreType.DMA((4,))],
        compiler_params=pltpu.CompilerParams(vmem_limit_bytes=4 * MIB),
    )(*tables)

    where = jnp.stack([lax.axis_index("z"), lax.axis_index("core")]).astype(jnp.int32)
    forward = [(i, (i + 1) % 8) for i in range(8)]
    backward = [(i, (i - 1) % 8) for i in range(8)]
    up = [amps[:, : depth // 2], amps[:, depth // 2 :]]
    down = list(up)
    pieces = list(up)
    for hop in range(3):
        up[0] = lax.ppermute(up[0], "z", forward)
        up[1] = lax.ppermute(up[1], "z", forward)
        down[0] = lax.ppermute(down[0], "z", backward)
        down[1] = lax.ppermute(down[1], "z", backward)
        if hop == 0:
            up[0], cd, where = lax.optimization_barrier((up[0], cd, where))
            high, ready = pl.pallas_call(
                high_kernel,
                out_shape=(half, lines),
                in_specs=[vmem, vmem, hbm, hbm, hbm],
                out_specs=(vmem, vmem),
                scratch_shapes=[pltpu.SemaphoreType.DMA((4,))],
                compiler_params=pltpu.CompilerParams(vmem_limit_bytes=4 * MIB),
            )(cd, ab, tables[-1], up[1], down[0])
        if hop == 1:
            up[0], ready = lax.optimization_barrier((up[0], ready))
        pieces += up + down
    last = [lax.ppermute(up[0], "z", forward), lax.ppermute(down[1], "z", backward)]
    size = rows * width // LANES
    first = pltpu.VMEM((14, size, LANES), jnp.float32)
    final = pltpu.VMEM((2, size, LANES), jnp.float32)
    keep, send = pl.pallas_call(
        first_kernel,
        out_shape=(first, first),
        grid_spec=pltpu.PrefetchScalarGridSpec(
            num_scalar_prefetch=1,
            grid=(),
            in_specs=[vmem] * 17,
            out_specs=(vmem, vmem),
            scratch_shapes=[pltpu.VMEM((7 * amps.shape[0], width), jnp.float32)],
        ),
        compiler_params=pltpu.CompilerParams(vmem_limit_bytes=8 * MIB),
    )(where, ready, low, high, *pieces)
    swap = [(0, 1), (1, 0)]
    send, *last = lax.optimization_barrier((send, *last))
    got = lax.ppermute(send, "core", swap)
    last_keep, last_send = pl.pallas_call(
        last_kernel,
        out_shape=(final, final),
        grid_spec=pltpu.PrefetchScalarGridSpec(
            num_scalar_prefetch=1,
            grid=(),
            in_specs=[vmem] * 4,
            out_specs=(vmem, vmem),
            scratch_shapes=[pltpu.VMEM((amps.shape[0], width), jnp.float32)],
        ),
        compiler_params=pltpu.CompilerParams(vmem_limit_bytes=8 * MIB),
    )(where, low, high, *last)
    last_got = lax.ppermute(last_send, "core", swap)
    packed = pl.pallas_call(
        pack_kernel,
        out_shape=pltpu.VMEM((16, size + 16, LANES), jnp.int16),
        grid_spec=pltpu.PrefetchScalarGridSpec(
            num_scalar_prefetch=1, grid=(), in_specs=[vmem] * 4, out_specs=vmem
        ),
        compiler_params=pltpu.CompilerParams(vmem_limit_bytes=4 * MIB),
    )(where, keep, got, last_keep, last_got)
    parts = lax.all_to_all(packed, ("y", "x"), 0, 0, tiled=True)
    return pl.pallas_call(
        finish_kernel,
        out_shape=jax.ShapeDtypeStruct((rows, width), jnp.float32),
        in_specs=[vmem] * 3,
        out_specs=vmem,
        compiler_params=pltpu.CompilerParams(vmem_limit_bytes=4 * MIB),
    )(parts, virt, occ)


def solution(mesh):
    fine = Mesh(mesh.devices.reshape(8, 4, 4, 2), ("z", "y", "x", "core"))
    col = ("y", "x", "core")
    in_specs = (
        P("z", col), P(col, "z"), P(col), P(col), P("z"), P("z"), P(col), P(col), P(), P(), P(),
    )
    return jax.shard_map(
        on_device, mesh=fine, in_specs=in_specs, out_specs=P(col, "z"), check_vma=False
    )
```

```python
import jax
import jax.numpy as jnp
from jax import lax
from jax.experimental import pallas as pl
from jax.experimental.pallas import tpu as pltpu
from jax.sharding import Mesh, PartitionSpec as P

LANES = 128
SHARDS = (0, -1, 1, -2, 2, -3, 3, 4)
MIB = 1024 * 1024


def lookup(table_ref, index):
    size = table_ref.shape[0]
    high = index // LANES
    low = index % LANES
    picked = jnp.zeros(index.shape, table_ref.dtype)
    for row in range(-(-size // LANES)):
        line = table_ref[pl.ds(row * LANES, min(LANES, size - row * LANES))].reshape(1, -1)
        if line.shape[1] < LANES:
            line = jnp.pad(line, ((0, 0), (0, LANES - line.shape[1])))
        line = jnp.broadcast_to(line, index.shape)
        value = jnp.take_along_axis(line, low, axis=1, mode="promise_in_bounds")
        picked = jnp.where(high == row, value, picked)
    return picked


def fetch(values, masked, arrived, first):
    blocks = arrived.shape[0]
    size = masked.shape[0] // blocks
    copies = []
    for block in range(blocks):
        copies.append(
            pltpu.make_async_copy(
                values.at[pl.ds(first + block * size, size), :],
                masked.at[pl.ds(block * size, size), :],
                arrived.at[block],
            )
        )
        copies[-1].start()
    return copies


def apply_mask(copies, masked, lines, other):
    size = masked.shape[0] // len(copies)
    other = [jnp.broadcast_to(other[i : i + 1, :], (LANES, LANES)) for i in range(other.shape[0])]
    for block, copy in enumerate(copies):
        copy.wait()
        for part in range(block * size // LANES, (block + 1) * size // LANES):
            label = jnp.broadcast_to(lines(part), (LANES, LANES)).T.astype(jnp.bfloat16)
            down = slice(part * LANES, part * LANES + LANES)
            for lane in range(masked.shape[1] // LANES):
                across = slice(lane * LANES, lane * LANES + LANES)
                piece = masked[down, across]
                masked[down, across] = jnp.where(
                    label == other[lane], piece, jnp.zeros_like(piece)
                )


def low_kernel(cd1, cd2, ab1, ab2, occ1, occ2, irrep, virt, energy, values, masked, cd_out, ab_out, virt_out, occ_out, arrived):
    copies = fetch(values, masked, arrived, 0)
    label = lookup(irrep, ab1[...]) ^ lookup(irrep, ab2[...])
    other = label.astype(jnp.float32)
    ab_out[...] = other
    labels = []
    for tile in range(cd1.shape[0] // 8):
        part = slice(8 * tile, 8 * tile + 8)
        label = lookup(irrep, cd1[part, :]) ^ lookup(irrep, cd2[part, :])
        labels.append(label.astype(jnp.float32))
    for tile in range(len(labels) // 2):
        cd_out[8 * tile : 8 * tile + 8, :] = labels[len(labels) // 2 + tile]
    virt_out[...] = lookup(virt, ab1[...]) + lookup(virt, ab2[...])
    for row in range(occ1.shape[0]):
        both = energy[occ1[row]] + energy[occ2[row]]
        occ_out[row : row + 1, :] = jnp.full((1, LANES), both, jnp.float32)
    lines = lambda part: labels[part // 8][part % 8 : part % 8 + 1, :]
    apply_mask(copies, masked, lines, other.astype(jnp.bfloat16))


def high_kernel(cd, ab, values, after1, after2, masked, ready, arrived):
    copies = fetch(values, masked, arrived, masked.shape[0])
    ready[...] = ab[...]
    lines = lambda part: cd[part : part + 1, :]
    apply_mask(copies, masked, lines, ab[...].astype(jnp.bfloat16))


def spread(where, total, place, rows, keep, send):
    first_core = where[1] == 0
    for high in range(2):
        at = place * 4 * rows + 2 * high * rows
        even = total[at : at + rows, :]
        odd = total[at + rows : at + 2 * rows, :]
        kept = jnp.where(first_core, even, odd)
        sent = jnp.where(first_core, odd, even)
        for lane in range(kept.shape[1] // LANES):
            across = slice(lane * LANES, lane * LANES + LANES)
            down = slice(lane * rows, lane * rows + rows)
            keep[2 * place + high, down, :] = kept[:, across]
            send[2 * place + high, down, :] = sent[:, across]


def ladder_kernel(where, ready, low, high, after1, after2, *refs):
    pieces = refs[:-3]
    keep, send, total = refs[-3:]
    left = jnp.concatenate([piece[...] for piece in pieces[0::2]], axis=0)
    right = jnp.concatenate([piece[...] for piece in pieces[1::2]], axis=0)
    total[...] = jnp.dot(left, low[...], preferred_element_type=jnp.float32)
    total[...] += jnp.dot(right, high[...], preferred_element_type=jnp.float32)
    for place in range(len(pieces) // 2):
        spread(where, total, place, pieces[0].shape[0] // 4, keep, send)


def ladder(where, ready, low, high, after, pieces):
    vmem = pl.BlockSpec(memory_space=pltpu.VMEM)
    hbm = pl.BlockSpec(memory_space=pl.ANY)
    count = len(pieces) // 2
    height, width = pieces[0].shape[0], low.shape[1]
    block = pltpu.VMEM((2 * count, height * width // 4 // LANES, LANES), jnp.float32)
    return pl.pallas_call(
        ladder_kernel,
        out_shape=(block, block),
        grid_spec=pltpu.PrefetchScalarGridSpec(
            num_scalar_prefetch=1,
            grid=(),
            in_specs=[vmem] * 3 + [hbm] * 2 + [vmem] * len(pieces),
            out_specs=(vmem, vmem),
            scratch_shapes=[pltpu.VMEM((count * height, width), jnp.float32)],
        ),
        compiler_params=pltpu.CompilerParams(vmem_limit_bytes=8 * MIB),
    )(where, ready, low, high, *after, *pieces)


def pack_kernel(where, *refs):
    out = refs[-1]
    kept, got = refs[: len(refs) // 2], refs[len(refs) // 2 : -1]
    rows = kept[0].shape[1]
    shifts = iter(SHARDS)
    for mine, other in zip(kept, got):
        for place in range(mine.shape[0] // 2):
            shard = lax.rem(where[0] + (next(shifts) + 8), 8)
            for high in range(2):
                both = mine[2 * place + high] + other[2 * place + high]
                top = jnp.maximum(jnp.max(jnp.abs(both), axis=0, keepdims=True), 1e-30)
                power = jnp.floor(14.99 - jnp.log2(top))
                scaled = jnp.clip(jnp.round(both * jnp.exp2(power)), -32767.0, 32767.0)
                out[2 * shard + high, :rows, :] = scaled.astype(jnp.int32).astype(jnp.int16)
                power = jnp.broadcast_to(power, (out.shape[1] - rows, LANES))
                out[2 * shard + high, rows:, :] = power.astype(jnp.int32).astype(jnp.int16)


def finish_kernel(parts, virt, occ, out):
    rows = out.shape[0]
    size = rows * out.shape[1] // LANES
    summed = jnp.zeros((size, LANES), jnp.float32)
    for block in range(parts.shape[0]):
        power = parts[block, size:, :].astype(jnp.int32).astype(jnp.float32)
        value = parts[block, :size, :].astype(jnp.int32).astype(jnp.float32)
        summed += value * jnp.exp2(-power[0:1, :])
    for lane in range(out.shape[1] // LANES):
        ladder = summed[lane * rows : lane * rows + rows, :]
        denom = virt[lane : lane + 1, :] - occ[:rows, :]
        out[:, lane * LANES : lane * LANES + LANES] = ladder / denom


def on_device(amps, integrals, cd1, cd2, ab1, ab2, occ1, occ2, irrep, occ_energy, virt_energy):
    depth = amps.shape[1]
    width = integrals.shape[1]
    rows = occ1.shape[0]
    vmem = pl.BlockSpec(memory_space=pltpu.VMEM)
    smem = pl.BlockSpec(memory_space=pltpu.SMEM)
    square = lambda x: x.reshape(x.shape[0] // LANES, LANES)
    tables = [pltpu.with_memory_space_constraint(x, pltpu.HBM) for x in (
        square(cd1), square(cd2), square(ab1), square(ab2), occ1, occ2,
        irrep, virt_energy, occ_energy, integrals,
    )]
    half = pltpu.VMEM((depth // 2, width), jnp.bfloat16)
    lines = pltpu.VMEM((width // LANES, LANES), jnp.float32)
    hbm = pl.BlockSpec(memory_space=pl.ANY)
    low, cd, ab, virt, occ = pl.pallas_call(
        low_kernel,
        out_shape=(
            half,
            pltpu.VMEM((depth // LANES // 2, LANES), jnp.float32),
            lines,
            lines,
            pltpu.VMEM((16, LANES), jnp.float32),
        ),
        in_specs=[vmem] * 4 + [smem] * 2 + [vmem] * 2 + [smem, hbm],
        out_specs=(vmem,) * 5,
        scratch_shapes=[pltpu.SemaphoreType.DMA((4,))],
        compiler_params=pltpu.CompilerParams(vmem_limit_bytes=4 * MIB),
    )(*tables)

    where = jnp.stack([lax.axis_index("z"), lax.axis_index("core")]).astype(jnp.int32)
    forward = [(i, (i + 1) % 8) for i in range(8)]
    backward = [(i, (i - 1) % 8) for i in range(8)]
    up = [amps[:, : depth // 2], amps[:, depth // 2 :]]
    down = list(up)
    pieces = list(up)
    for hop in range(3):
        up[0] = lax.ppermute(up[0], "z", forward)
        up[1] = lax.ppermute(up[1], "z", forward)
        down[0] = lax.ppermute(down[0], "z", backward)
        down[1] = lax.ppermute(down[1], "z", backward)
        if hop == 0:
            up[0], cd, where = lax.optimization_barrier((up[0], cd, where))
            high, ready = pl.pallas_call(
                high_kernel,
                out_shape=(half, lines),
                in_specs=[vmem, vmem, hbm, hbm, hbm],
                out_specs=(vmem, vmem),
                scratch_shapes=[pltpu.SemaphoreType.DMA((4,))],
                compiler_params=pltpu.CompilerParams(vmem_limit_bytes=4 * MIB),
            )(cd, ab, tables[-1], up[1], down[0])
        if hop == 1:
            up[0], ready = lax.optimization_barrier((up[0], ready))
        pieces += up + down
    last = [lax.ppermute(up[0], "z", forward), lax.ppermute(down[1], "z", backward)]
    swap = [(0, 1), (1, 0)]
    after = [up[0], down[1]]
    keep1, send1 = ladder(where, ready, low, high, after, pieces[:10])
    keep2, send2 = ladder(where, ready, low, high, after, pieces[10:])
    send1, send2, *last = lax.optimization_barrier((send1, send2, *last))
    got1, got2 = lax.ppermute(send1, "core", swap), lax.ppermute(send2, "core", swap)
    keep3, send3 = ladder(where, ready, low, high, after, last)
    got3 = lax.ppermute(send3, "core", swap)
    packed = pl.pallas_call(
        pack_kernel,
        out_shape=pltpu.VMEM((16, rows * width // LANES + 16, LANES), jnp.int16),
        grid_spec=pltpu.PrefetchScalarGridSpec(
            num_scalar_prefetch=1, grid=(), in_specs=[vmem] * 6, out_specs=vmem
        ),
        compiler_params=pltpu.CompilerParams(vmem_limit_bytes=4 * MIB),
    )(where, keep1, keep2, keep3, got1, got2, got3)
    parts = lax.all_to_all(packed, ("y", "x"), 0, 0, tiled=True)
    return pl.pallas_call(
        finish_kernel,
        out_shape=jax.ShapeDtypeStruct((rows, width), jnp.float32),
        in_specs=[vmem] * 3,
        out_specs=vmem,
        compiler_params=pltpu.CompilerParams(vmem_limit_bytes=4 * MIB),
    )(parts, virt, occ)


def solution(mesh):
    fine = Mesh(mesh.devices.reshape(8, 4, 4, 2), ("z", "y", "x", "core"))
    col = ("y", "x", "core")
    in_specs = (
        P("z", col), P(col, "z"), P(col), P(col), P("z"), P("z"), P(col), P(col), P(), P(), P(),
    )
    return jax.shard_map(
        on_device, mesh=fine, in_specs=in_specs, out_specs=P(col, "z"), check_vma=False
    )
```

```python
import jax
import jax.numpy as jnp
from jax import lax
from jax.experimental import pallas as pl
from jax.experimental.pallas import tpu as pltpu
from jax.sharding import Mesh, PartitionSpec as P

LANES = 128
SHARDS = (0, -1, 1, -2, 2, -3, 3, 4)
MIB = 1024 * 1024


def lookup(table_ref, index):
    size = table_ref.shape[0]
    high = index // LANES
    low = index % LANES
    picked = jnp.zeros(index.shape, table_ref.dtype)
    for row in range(-(-size // LANES)):
        line = table_ref[pl.ds(row * LANES, min(LANES, size - row * LANES))].reshape(1, -1)
        if line.shape[1] < LANES:
            line = jnp.pad(line, ((0, 0), (0, LANES - line.shape[1])))
        line = jnp.broadcast_to(line, index.shape)
        value = jnp.take_along_axis(line, low, axis=1, mode="promise_in_bounds")
        picked = jnp.where(high == row, value, picked)
    return picked


def fetch(values, masked, arrived, first):
    blocks = arrived.shape[0]
    size = masked.shape[0] // blocks
    copies = []
    for block in range(blocks):
        copies.append(
            pltpu.make_async_copy(
                values.at[pl.ds(first + block * size, size), :],
                masked.at[pl.ds(block * size, size), :],
                arrived.at[block],
            )
        )
        copies[-1].start()
    return copies


def apply_mask(copies, masked, lines, other):
    size = masked.shape[0] // len(copies)
    other = [jnp.broadcast_to(other[i : i + 1, :], (LANES, LANES)) for i in range(other.shape[0])]
    for block, copy in enumerate(copies):
        copy.wait()
        for part in range(block * size // LANES, (block + 1) * size // LANES):
            label = jnp.broadcast_to(lines(part), (LANES, LANES)).T.astype(jnp.bfloat16)
            down = slice(part * LANES, part * LANES + LANES)
            for lane in range(masked.shape[1] // LANES):
                across = slice(lane * LANES, lane * LANES + LANES)
                piece = masked[down, across]
                masked[down, across] = jnp.where(
                    label == other[lane], piece, jnp.zeros_like(piece)
                )


def low_kernel(cd1, cd2, ab1, ab2, occ1, occ2, irrep, virt, energy, values, masked, cd_out, ab_out, virt_out, occ_out, arrived):
    copies = fetch(values, masked, arrived, 0)
    label = lookup(irrep, ab1[...]) ^ lookup(irrep, ab2[...])
    other = label.astype(jnp.float32)
    ab_out[...] = other
    labels = []
    for tile in range(cd1.shape[0] // 8):
        part = slice(8 * tile, 8 * tile + 8)
        label = lookup(irrep, cd1[part, :]) ^ lookup(irrep, cd2[part, :])
        labels.append(label.astype(jnp.float32))
    for tile in range(len(labels) // 2):
        cd_out[8 * tile : 8 * tile + 8, :] = labels[len(labels) // 2 + tile]
    virt_out[...] = lookup(virt, ab1[...]) + lookup(virt, ab2[...])
    for row in range(occ1.shape[0]):
        both = energy[occ1[row]] + energy[occ2[row]]
        occ_out[row : row + 1, :] = jnp.full((1, LANES), both, jnp.float32)
    lines = lambda part: labels[part // 8][part % 8 : part % 8 + 1, :]
    apply_mask(copies, masked, lines, other.astype(jnp.bfloat16))


def high_kernel(cd, ab, values, after1, after2, masked, ready, arrived):
    copies = fetch(values, masked, arrived, masked.shape[0])
    ready[...] = ab[...]
    lines = lambda part: cd[part : part + 1, :]
    apply_mask(copies, masked, lines, ab[...].astype(jnp.bfloat16))


def spread(where, total, place, rows, keep, send):
    first_core = where[1] == 0
    for high in range(2):
        at = place * 4 * rows + 2 * high * rows
        even = total[at : at + rows, :]
        odd = total[at + rows : at + 2 * rows, :]
        kept = jnp.where(first_core, even, odd)
        sent = jnp.where(first_core, odd, even)
        for lane in range(kept.shape[1] // LANES):
            across = slice(lane * LANES, lane * LANES + LANES)
            down = slice(lane * rows, lane * rows + rows)
            keep[2 * place + high, down, :] = kept[:, across]
            send[2 * place + high, down, :] = sent[:, across]


def ladder_kernel(where, ready, low, high, after1, after2, *refs):
    pieces = refs[:-3]
    keep, send, total = refs[-3:]
    left = jnp.concatenate([piece[...] for piece in pieces[0::2]], axis=0)
    right = jnp.concatenate([piece[...] for piece in pieces[1::2]], axis=0)
    total[...] = jnp.dot(left, low[...], preferred_element_type=jnp.float32)
    total[...] += jnp.dot(right, high[...], preferred_element_type=jnp.float32)
    for place in range(len(pieces) // 2):
        spread(where, total, place, pieces[0].shape[0] // 4, keep, send)


def ladder(where, ready, low, high, after, pieces):
    vmem = pl.BlockSpec(memory_space=pltpu.VMEM)
    hbm = pl.BlockSpec(memory_space=pl.ANY)
    count = len(pieces) // 2
    height, width = pieces[0].shape[0], low.shape[1]
    block = pltpu.VMEM((2 * count, height * width // 4 // LANES, LANES), jnp.float32)
    return pl.pallas_call(
        ladder_kernel,
        out_shape=(block, block),
        grid_spec=pltpu.PrefetchScalarGridSpec(
            num_scalar_prefetch=1,
            grid=(),
            in_specs=[vmem] * 3 + [hbm] * 2 + [vmem] * len(pieces),
            out_specs=(vmem, vmem),
            scratch_shapes=[pltpu.VMEM((count * height, width), jnp.float32)],
        ),
        compiler_params=pltpu.CompilerParams(vmem_limit_bytes=8 * MIB),
    )(where, ready, low, high, *after, *pieces)


def touch_kernel(ready, after1, after2, after3, out):
    out[...] = ready[...]


def pack_kernel(where, first_keep, last_keep, first_got, last_got, out):
    rows = first_keep.shape[1]
    first = first_keep.shape[0] // 2
    for place, shift in enumerate(SHARDS):
        shard = lax.rem(where[0] + (shift + 8), 8)
        for high in range(2):
            if place < first:
                both = first_keep[2 * place + high] + first_got[2 * place + high]
            else:
                at = 2 * (place - first) + high
                both = last_keep[at] + last_got[at]
            top = jnp.maximum(jnp.max(jnp.abs(both), axis=0, keepdims=True), 1e-30)
            power = jnp.floor(14.99 - jnp.log2(top))
            scaled = jnp.clip(jnp.round(both * jnp.exp2(power)), -32767.0, 32767.0)
            out[2 * shard + high, :rows, :] = scaled.astype(jnp.int32).astype(jnp.int16)
            power = jnp.broadcast_to(power, (out.shape[1] - rows, LANES))
            out[2 * shard + high, rows:, :] = power.astype(jnp.int32).astype(jnp.int16)


def finish_kernel(parts, virt, occ, out):
    rows = out.shape[0]
    size = rows * out.shape[1] // LANES
    summed = jnp.zeros((size, LANES), jnp.float32)
    for block in range(parts.shape[0]):
        power = parts[block, size:, :].astype(jnp.int32).astype(jnp.float32)
        value = parts[block, :size, :].astype(jnp.int32).astype(jnp.float32)
        summed += value * jnp.exp2(-power[0:1, :])
    for lane in range(out.shape[1] // LANES):
        ladder = summed[lane * rows : lane * rows + rows, :]
        denom = virt[lane : lane + 1, :] - occ[:rows, :]
        out[:, lane * LANES : lane * LANES + LANES] = ladder / denom


def on_device(amps, integrals, cd1, cd2, ab1, ab2, occ1, occ2, irrep, occ_energy, virt_energy):
    depth = amps.shape[1]
    width = integrals.shape[1]
    rows = occ1.shape[0]
    vmem = pl.BlockSpec(memory_space=pltpu.VMEM)
    smem = pl.BlockSpec(memory_space=pltpu.SMEM)
    square = lambda x: x.reshape(x.shape[0] // LANES, LANES)
    tables = [pltpu.with_memory_space_constraint(x, pltpu.HBM) for x in (
        square(cd1), square(cd2), square(ab1), square(ab2), occ1, occ2,
        irrep, virt_energy, occ_energy, integrals,
    )]
    half = pltpu.VMEM((depth // 2, width), jnp.bfloat16)
    lines = pltpu.VMEM((width // LANES, LANES), jnp.float32)
    hbm = pl.BlockSpec(memory_space=pl.ANY)
    low, cd, ab, virt, occ = pl.pallas_call(
        low_kernel,
        out_shape=(
            half,
            pltpu.VMEM((depth // LANES // 2, LANES), jnp.float32),
            lines,
            lines,
            pltpu.VMEM((16, LANES), jnp.float32),
        ),
        in_specs=[vmem] * 4 + [smem] * 2 + [vmem] * 2 + [smem, hbm],
        out_specs=(vmem,) * 5,
        scratch_shapes=[pltpu.SemaphoreType.DMA((4,))],
        compiler_params=pltpu.CompilerParams(vmem_limit_bytes=4 * MIB),
    )(*tables)

    where = jnp.stack([lax.axis_index("z"), lax.axis_index("core")]).astype(jnp.int32)
    forward = [(i, (i + 1) % 8) for i in range(8)]
    backward = [(i, (i - 1) % 8) for i in range(8)]
    up = [amps[:, : depth // 2], amps[:, depth // 2 :]]
    down = list(up)
    pieces = list(up)
    for hop in range(3):
        up[0] = lax.ppermute(up[0], "z", forward)
        up[1] = lax.ppermute(up[1], "z", forward)
        down[0] = lax.ppermute(down[0], "z", backward)
        down[1] = lax.ppermute(down[1], "z", backward)
        if hop == 0:
            up[0], cd, where = lax.optimization_barrier((up[0], cd, where))
            high, ready = pl.pallas_call(
                high_kernel,
                out_shape=(half, lines),
                in_specs=[vmem, vmem, hbm, hbm, hbm],
                out_specs=(vmem, vmem),
                scratch_shapes=[pltpu.SemaphoreType.DMA((4,))],
                compiler_params=pltpu.CompilerParams(vmem_limit_bytes=4 * MIB),
            )(cd, ab, tables[-1], up[1], down[0])
        if hop == 1:
            up[0], ready = lax.optimization_barrier((up[0], ready))
        pieces += up + down
    last = [lax.ppermute(up[0], "z", forward), lax.ppermute(down[1], "z", backward)]
    swap = [(0, 1), (1, 0)]
    after = [up[0], down[1]]
    keep, send = ladder(where, ready, low, high, after, pieces[:10])
    touched = pl.pallas_call(
        touch_kernel,
        out_shape=lines,
        in_specs=[vmem, hbm, hbm, hbm],
        out_specs=vmem,
        compiler_params=pltpu.CompilerParams(vmem_limit_bytes=1 * MIB),
    )(ready, up[1], down[0], keep)
    send, ready, *last = lax.optimization_barrier((send, touched, *last))
    got = lax.ppermute(send, "core", swap)
    last_keep, last_send = ladder(where, ready, low, high, after, pieces[10:] + last)
    last_got = lax.ppermute(last_send, "core", swap)
    packed = pl.pallas_call(
        pack_kernel,
        out_shape=pltpu.VMEM((16, rows * width // LANES + 16, LANES), jnp.int16),
        grid_spec=pltpu.PrefetchScalarGridSpec(
            num_scalar_prefetch=1, grid=(), in_specs=[vmem] * 4, out_specs=vmem
        ),
        compiler_params=pltpu.CompilerParams(vmem_limit_bytes=4 * MIB),
    )(where, keep, last_keep, got, last_got)
    parts = lax.all_to_all(packed, ("y", "x"), 0, 0, tiled=True)
    return pl.pallas_call(
        finish_kernel,
        out_shape=jax.ShapeDtypeStruct((rows, width), jnp.float32),
        in_specs=[vmem] * 3,
        out_specs=vmem,
        compiler_params=pltpu.CompilerParams(vmem_limit_bytes=4 * MIB),
    )(parts, virt, occ)


def solution(mesh):
    fine = Mesh(mesh.devices.reshape(8, 4, 4, 2), ("z", "y", "x", "core"))
    col = ("y", "x", "core")
    in_specs = (
        P("z", col), P(col, "z"), P(col), P(col), P("z"), P("z"), P(col), P(col), P(), P(), P(),
    )
    return jax.shard_map(
        on_device, mesh=fine, in_specs=in_specs, out_specs=P(col, "z"), check_vma=False
    )
```

```python
import jax
import jax.numpy as jnp
from jax import lax
from jax.experimental import pallas as pl
from jax.experimental.pallas import tpu as pltpu
from jax.sharding import Mesh, PartitionSpec as P

LANES = 128
SHARDS = (0, -1, 1, -2, 2, -3, 3, 4)
MIB = 1024 * 1024


def lookup(table_ref, index):
    size = table_ref.shape[0]
    high = index // LANES
    low = index % LANES
    picked = jnp.zeros(index.shape, table_ref.dtype)
    for row in range(-(-size // LANES)):
        line = table_ref[pl.ds(row * LANES, min(LANES, size - row * LANES))].reshape(1, -1)
        if line.shape[1] < LANES:
            line = jnp.pad(line, ((0, 0), (0, LANES - line.shape[1])))
        line = jnp.broadcast_to(line, index.shape)
        value = jnp.take_along_axis(line, low, axis=1, mode="promise_in_bounds")
        picked = jnp.where(high == row, value, picked)
    return picked


def fetch(values, masked, arrived, first):
    blocks = arrived.shape[0]
    size = masked.shape[0] // blocks
    copies = []
    for block in range(blocks):
        copies.append(
            pltpu.make_async_copy(
                values.at[pl.ds(first + block * size, size), :],
                masked.at[pl.ds(block * size, size), :],
                arrived.at[block],
            )
        )
        copies[-1].start()
    return copies


def apply_mask(copies, masked, lines, other):
    size = masked.shape[0] // len(copies)
    other = [jnp.broadcast_to(other[i : i + 1, :], (LANES, LANES)) for i in range(other.shape[0])]
    for block, copy in enumerate(copies):
        copy.wait()
        for part in range(block * size // LANES, (block + 1) * size // LANES):
            label = jnp.broadcast_to(lines(part), (LANES, LANES)).T.astype(jnp.bfloat16)
            down = slice(part * LANES, part * LANES + LANES)
            for lane in range(masked.shape[1] // LANES):
                across = slice(lane * LANES, lane * LANES + LANES)
                piece = masked[down, across]
                masked[down, across] = jnp.where(
                    label == other[lane], piece, jnp.zeros_like(piece)
                )


def low_kernel(cd1, cd2, ab1, ab2, occ1, occ2, irrep, virt, energy, values, masked, cd_out, ab_out, virt_out, occ_out, arrived):
    copies = fetch(values, masked, arrived, 0)
    label = lookup(irrep, ab1[...]) ^ lookup(irrep, ab2[...])
    other = label.astype(jnp.float32)
    ab_out[...] = other
    labels = []
    for tile in range(cd1.shape[0] // 8):
        part = slice(8 * tile, 8 * tile + 8)
        label = lookup(irrep, cd1[part, :]) ^ lookup(irrep, cd2[part, :])
        labels.append(label.astype(jnp.float32))
    for tile in range(len(labels) // 2):
        cd_out[8 * tile : 8 * tile + 8, :] = labels[len(labels) // 2 + tile]
    virt_out[...] = lookup(virt, ab1[...]) + lookup(virt, ab2[...])
    for row in range(occ1.shape[0]):
        both = energy[occ1[row]] + energy[occ2[row]]
        occ_out[row : row + 1, :] = jnp.full((1, LANES), both, jnp.float32)
    lines = lambda part: labels[part // 8][part % 8 : part % 8 + 1, :]
    apply_mask(copies, masked, lines, other.astype(jnp.bfloat16))


def high_kernel(cd, ab, values, after1, after2, masked, ready, arrived):
    copies = fetch(values, masked, arrived, masked.shape[0])
    ready[...] = ab[...]
    lines = lambda part: cd[part : part + 1, :]
    apply_mask(copies, masked, lines, ab[...].astype(jnp.bfloat16))


def spread(where, total, place, rows, keep, send):
    first_core = where[1] == 0
    for high in range(2):
        at = place * 4 * rows + 2 * high * rows
        even = total[at : at + rows, :]
        odd = total[at + rows : at + 2 * rows, :]
        kept = jnp.where(first_core, even, odd)
        sent = jnp.where(first_core, odd, even)
        for lane in range(kept.shape[1] // LANES):
            across = slice(lane * LANES, lane * LANES + LANES)
            down = slice(lane * rows, lane * rows + rows)
            keep[2 * place + high, down, :] = kept[:, across]
            send[2 * place + high, down, :] = sent[:, across]


def ladder_kernel(where, ready, low, high, after1, after2, *refs):
    pieces = refs[:-3]
    keep, send, total = refs[-3:]
    left = jnp.concatenate([piece[...] for piece in pieces[0::2]], axis=0)
    right = jnp.concatenate([piece[...] for piece in pieces[1::2]], axis=0)
    total[...] = jnp.dot(left, low[...], preferred_element_type=jnp.float32)
    total[...] += jnp.dot(right, high[...], preferred_element_type=jnp.float32)
    for place in range(len(pieces) // 2):
        spread(where, total, place, pieces[0].shape[0] // 4, keep, send)


def ladder(where, ready, low, high, after, pieces):
    vmem = pl.BlockSpec(memory_space=pltpu.VMEM)
    hbm = pl.BlockSpec(memory_space=pl.ANY)
    count = len(pieces) // 2
    height, width = pieces[0].shape[0], low.shape[1]
    block = pltpu.VMEM((2 * count, height * width // 4 // LANES, LANES), jnp.float32)
    return pl.pallas_call(
        ladder_kernel,
        out_shape=(block, block),
        grid_spec=pltpu.PrefetchScalarGridSpec(
            num_scalar_prefetch=1,
            grid=(),
            in_specs=[vmem] * 3 + [hbm] * 2 + [vmem] * len(pieces),
            out_specs=(vmem, vmem),
            scratch_shapes=[pltpu.VMEM((count * height, width), jnp.float32)],
        ),
        compiler_params=pltpu.CompilerParams(vmem_limit_bytes=8 * MIB),
    )(where, ready, low, high, *after, *pieces)


def touch_kernel(ready, after1, after2, after3, out):
    out[...] = ready[...]


def pack_kernel(where, first_keep, last_keep, first_got, last_got, out):
    rows = first_keep.shape[1]
    first = first_keep.shape[0] // 2
    for place, shift in enumerate(SHARDS):
        shard = lax.rem(where[0] + (shift + 8), 8)
        for high in range(2):
            if place < first:
                both = first_keep[2 * place + high] + first_got[2 * place + high]
            else:
                at = 2 * (place - first) + high
                both = last_keep[at] + last_got[at]
            top = jnp.maximum(jnp.max(jnp.abs(both), axis=0, keepdims=True), 1e-30)
            power = jnp.floor(14.99 - jnp.log2(top))
            scaled = jnp.clip(jnp.round(both * jnp.exp2(power)), -32767.0, 32767.0)
            out[2 * shard + high, :rows, :] = scaled.astype(jnp.int32).astype(jnp.int16)
            power = jnp.broadcast_to(power, (out.shape[1] - rows, LANES))
            out[2 * shard + high, rows:, :] = power.astype(jnp.int32).astype(jnp.int16)


def finish_kernel(parts, virt, occ, out):
    rows = out.shape[0]
    size = rows * out.shape[1] // LANES
    summed = jnp.zeros((size, LANES), jnp.float32)
    for block in range(parts.shape[0]):
        power = parts[block, size:, :].astype(jnp.int32).astype(jnp.float32)
        value = parts[block, :size, :].astype(jnp.int32).astype(jnp.float32)
        summed += value * jnp.exp2(-power[0:1, :])
    for lane in range(out.shape[1] // LANES):
        ladder = summed[lane * rows : lane * rows + rows, :]
        denom = virt[lane : lane + 1, :] - occ[:rows, :]
        out[:, lane * LANES : lane * LANES + LANES] = ladder / denom


def on_device(amps, integrals, cd1, cd2, ab1, ab2, occ1, occ2, irrep, occ_energy, virt_energy):
    depth = amps.shape[1]
    width = integrals.shape[1]
    rows = occ1.shape[0]
    vmem = pl.BlockSpec(memory_space=pltpu.VMEM)
    smem = pl.BlockSpec(memory_space=pltpu.SMEM)
    square = lambda x: x.reshape(x.shape[0] // LANES, LANES)
    tables = [pltpu.with_memory_space_constraint(x, pltpu.HBM) for x in (
        square(cd1), square(cd2), square(ab1), square(ab2), occ1, occ2,
        irrep, virt_energy, occ_energy, integrals,
    )]
    half = pltpu.VMEM((depth // 2, width), jnp.bfloat16)
    lines = pltpu.VMEM((width // LANES, LANES), jnp.float32)
    hbm = pl.BlockSpec(memory_space=pl.ANY)
    low, cd, ab, virt, occ = pl.pallas_call(
        low_kernel,
        out_shape=(
            half,
            pltpu.VMEM((depth // LANES // 2, LANES), jnp.float32),
            lines,
            lines,
            pltpu.VMEM((16, LANES), jnp.float32),
        ),
        in_specs=[vmem] * 4 + [smem] * 2 + [vmem] * 2 + [smem, hbm],
        out_specs=(vmem,) * 5,
        scratch_shapes=[pltpu.SemaphoreType.DMA((4,))],
        compiler_params=pltpu.CompilerParams(vmem_limit_bytes=4 * MIB),
    )(*tables)

    where = jnp.stack([lax.axis_index("z"), lax.axis_index("core")]).astype(jnp.int32)
    forward = [(i, (i + 1) % 8) for i in range(8)]
    backward = [(i, (i - 1) % 8) for i in range(8)]
    up = [amps[:, : depth // 2], amps[:, depth // 2 :]]
    down = list(up)
    pieces = list(up)
    for hop in range(3):
        up[0] = lax.ppermute(up[0], "z", forward)
        up[1] = lax.ppermute(up[1], "z", forward)
        down[0] = lax.ppermute(down[0], "z", backward)
        down[1] = lax.ppermute(down[1], "z", backward)
        if hop == 0:
            up[0], cd, where = lax.optimization_barrier((up[0], cd, where))
        if hop == 1:
            high, ready = pl.pallas_call(
                high_kernel,
                out_shape=(half, lines),
                in_specs=[vmem, vmem, hbm, hbm, hbm],
                out_specs=(vmem, vmem),
                scratch_shapes=[pltpu.SemaphoreType.DMA((4,))],
                compiler_params=pltpu.CompilerParams(vmem_limit_bytes=4 * MIB),
            )(cd, ab, tables[-1], up[1], down[0])
        if hop == 2:
            up[0], ready = lax.optimization_barrier((up[0], ready))
        pieces += up + down
    last = [lax.ppermute(up[0], "z", forward), lax.ppermute(down[1], "z", backward)]
    swap = [(0, 1), (1, 0)]
    after = [up[0], down[1]]
    keep, send = ladder(where, ready, low, high, after, pieces[:10])
    touched = pl.pallas_call(
        touch_kernel,
        out_shape=lines,
        in_specs=[vmem, hbm, hbm, hbm],
        out_specs=vmem,
        compiler_params=pltpu.CompilerParams(vmem_limit_bytes=1 * MIB),
    )(ready, up[1], down[0], keep)
    send, ready, *last = lax.optimization_barrier((send, touched, *last))
    got = lax.ppermute(send, "core", swap)
    last_keep, last_send = ladder(where, ready, low, high, after, pieces[10:] + last)
    last_got = lax.ppermute(last_send, "core", swap)
    packed = pl.pallas_call(
        pack_kernel,
        out_shape=pltpu.VMEM((16, rows * width // LANES + 16, LANES), jnp.int16),
        grid_spec=pltpu.PrefetchScalarGridSpec(
            num_scalar_prefetch=1, grid=(), in_specs=[vmem] * 4, out_specs=vmem
        ),
        compiler_params=pltpu.CompilerParams(vmem_limit_bytes=4 * MIB),
    )(where, keep, last_keep, got, last_got)
    parts = lax.all_to_all(packed, ("y", "x"), 0, 0, tiled=True)
    return pl.pallas_call(
        finish_kernel,
        out_shape=jax.ShapeDtypeStruct((rows, width), jnp.float32),
        in_specs=[vmem] * 3,
        out_specs=vmem,
        compiler_params=pltpu.CompilerParams(vmem_limit_bytes=4 * MIB),
    )(parts, virt, occ)


def solution(mesh):
    fine = Mesh(mesh.devices.reshape(8, 4, 4, 2), ("z", "y", "x", "core"))
    col = ("y", "x", "core")
    in_specs = (
        P("z", col), P(col, "z"), P(col), P(col), P("z"), P("z"), P(col), P(col), P(), P(), P(),
    )
    return jax.shard_map(
        on_device, mesh=fine, in_specs=in_specs, out_specs=P(col, "z"), check_vma=False
    )
```
